256 devices in a mesh: gz: 4 (over z_hi, core), subj: 64 (over x, z_lo, y).
Axes of the slice: x: 4, y: 4, z: 8 (z_hi: 2, z_lo: 4; z = z_hi * 4 + z_lo), core: 2. Of those that a mesh axis runs over, the one named last changes fastest.
Arguments:
- template: bfloat16 [256, 8, 128], P(('gz', 'subj')), may hold values from -6 to 6
- subjects: bfloat16 [64, 256, 8, 128], P('subj', 'gz'), may hold values from -16 to 16
- shifts: int32 [64, 3, 256, 8, 128], P('subj', None, 'gz'), may hold values from -2 to 2
- fractions: bfloat16 [64, 3, 256, 8, 128], P('subj', None, 'gz'), may hold values from 0 to 1
Outputs:
- velocity_step: float32 [64, 3, 256, 8, 128], P('subj', None, 'gz')
- template_force: float32 [256, 8, 128], P(('gz', 'subj'))
The draws below stay inside these ranges and needn't reach their ends.
All inputs are finite; a program needn't handle non-finite values.
Results may differ from the reference program's by a relative error of at most 0.0029.
Values may be sent and summed in bfloat16 or wider, within the bound.
A program may use at most 64 MiB of HBM per device.

```python
import math
import jax
import jax.numpy as jnp
from jax import lax

X = 8
Y = 128
SHIFT = 2
WIN = 4
SMOOTH = 4
SUBJECTS = 64
NZ = 256


def plant(result, own_key, least, top_value):
    shape = result.shape
    spot = [jax.random.randint(jax.random.fold_in(own_key, axis), (), 0, shape[axis]) for axis in range(len(shape))]
    result = result.at[tuple(spot)].set(least)
    longest = shape.index(max(shape))
    spot[longest] = (spot[longest] + 1) % shape[longest]
    return result.at[tuple(spot)].set(top_value)


def strengthened(entries, own_key, source, target, shards_of, factor):
    owner, partner = [(jnp.arange(entries.shape[dim]) // (entries.shape[dim] // shards_of)).reshape([-1 if axis == dim else 1 for axis in range(entries.ndim)]) for dim in (source, target)]
    chosen = jax.random.permutation(own_key, shards_of)[partner]
    strong = (owner == chosen) | (owner == (partner + shards_of // 2) % shards_of)
    return jnp.where(strong, factor * entries, entries)


def steps_of(key, shape, pieces, least, top_value):
    def one(dim, blocks):
        heights = jax.random.uniform(jax.random.fold_in(jax.random.fold_in(key, 6), dim), (blocks,), jnp.float32, least / len(pieces), top_value / len(pieces))
        return jnp.repeat(jnp.exp(heights), shape[dim] // blocks).reshape((-1,) + (1,) * (len(shape) - dim - 1))

    level = one(*pieces[0])
    for cut in pieces[1:]:
        level = level * one(*cut)
    return level


def bell_draw(own_key, shape, scale, most, shards=(), kind=jnp.bfloat16):
    level = steps_of(own_key, shape, shards, -0.22, 0.18) if shards else 1.0
    result = jax.random.normal(own_key, shape, jnp.float32) * scale * level
    return jnp.minimum(jnp.maximum(result, -most), most).astype(kind)


def gaussian_with(rng, extent, scale, limit, shards, heavy, kind=jnp.bfloat16):
    entries = scale * jax.random.normal(rng, extent, jnp.float32)
    if shards:
        entries = entries * steps_of(rng, extent, shards, -0.22, 0.18)
    return jnp.clip(strengthened(entries, jax.random.fold_in(rng, 3), *heavy), -limit, limit).astype(kind)


def setup_inputs(seed: int = 0) -> dict:
    splits = jax.random.split(jax.random.key(seed), 5)
    template = bell_draw(splits[0], (NZ, X, Y), 1.0, 6.0, ((0, 256),))
    subjects = gaussian_with(splits[1], (SUBJECTS, NZ, X, Y), 1.0, 16.0, ((0, 64), (1, 4)), (0, 1, 64, 4.0))
    shifts = plant(jax.random.randint(splits[2], (SUBJECTS, 3, NZ, X, Y), 0 - SHIFT, SHIFT + 1), jax.random.fold_in(splits[2], 1), 0 - SHIFT, SHIFT).astype(jnp.int32)
    fractions = jnp.clip(1.0 * jax.random.uniform(splits[3], (SUBJECTS, 3, NZ, X, Y), jnp.float32) ** steps_of(splits[3], (SUBJECTS, 3, NZ, X, Y), ((0, 64), (2, 4)), -0.2, 0.2), 0.0, 1.0).astype(jnp.bfloat16)
    return dict(template=template, subjects=subjects, shifts=shifts, fractions=fractions)


sigma = 1.5
epsilon = 1e-05
highest = lax.Precision.HIGHEST

def gauss_norm():
    offsets = jnp.arange(-SMOOTH, SMOOTH + 1, dtype=jnp.int32).astype(jnp.float32)
    return jnp.sum(jnp.exp(-0.5 * offsets * offsets / (sigma * sigma)))

def gauss_taps():
    offsets = jnp.arange(-SMOOTH, SMOOTH + 1, dtype=jnp.int32).astype(jnp.float32)
    return jnp.exp(-0.5 * offsets * offsets / (sigma * sigma)) / gauss_norm()

def band_matrix(length, radius):
    places = jnp.arange(length, dtype=jnp.int32)
    apart = places[:, None] - places[None, :]
    return (jnp.abs(apart) <= radius).astype(jnp.float32)

def gauss_matrix(length):
    places = jnp.arange(length, dtype=jnp.int32)
    apart = places[:, None] - places[None, :]
    offsets = apart.astype(jnp.float32)
    values = jnp.exp(-0.5 * offsets * offsets / (sigma * sigma)) / gauss_norm()
    return jnp.where(jnp.abs(apart) <= SMOOTH, values, jnp.zeros_like(values))

def inplane(fields, row_matrix, col_matrix):
    mixed = jnp.einsum('...xy,yv->...xv', fields, col_matrix, precision=highest)
    return jnp.einsum('...xy,xu->...uy', mixed, row_matrix, precision=highest)

def zwindow(fields, length, taps):
    summed = taps[0] * fields[..., 0:length, :, :]
    for offset in range(1, taps.shape[0]):
        summed = summed + taps[offset] * fields[..., offset:offset + length, :, :]
    return summed

def warp(padded_template, front, shift_one, frac_one):
    depth_len, row_len, col_len = frac_one.shape[1:]
    depth_index = jnp.arange(depth_len, dtype=jnp.int32)[:, None, None] + shift_one[0] + front
    row_index = jnp.arange(row_len, dtype=jnp.int32)[None, :, None] + shift_one[1] + SHIFT
    col_index = jnp.arange(col_len, dtype=jnp.int32)[None, None, :] + shift_one[2] + SHIFT
    flat_values = padded_template.reshape(-1)
    row_stride = padded_template.shape[1]
    col_stride = padded_template.shape[2]
    weights = frac_one.astype(jnp.float32)
    summed = jnp.zeros(frac_one.shape[1:], jnp.float32)
    for a in (0, 1):
        weight_depth = weights[0] if a else 1.0 - weights[0]
        for b in (0, 1):
            weight_row = weights[1] if b else 1.0 - weights[1]
            for e in (0, 1):
                weight_col = weights[2] if e else 1.0 - weights[2]
                position = ((depth_index + a) * row_stride + row_index + b) * col_stride + col_index + e
                summed = summed + weight_depth * weight_row * weight_col * jnp.take(flat_values, position)
    return lax.optimization_barrier(summed.astype(jnp.bfloat16))

def correlation_force(warped_ext, subject_ext, length):
    row_count = warped_ext.shape[-2]
    col_count = warped_ext.shape[-1]
    stacked = jnp.stack([warped_ext, subject_ext, warped_ext * warped_ext, subject_ext * subject_ext, warped_ext * subject_ext])
    box_sums = inplane(stacked, band_matrix(row_count, WIN), band_matrix(col_count, WIN))
    window = float((2 * WIN + 1) ** 3)
    local_means = zwindow(box_sums, length, jnp.ones((2 * WIN + 1,), jnp.float32)) / window
    centre_warped = warped_ext[..., WIN:WIN + length, :, :]
    centre_subject = subject_ext[..., WIN:WIN + length, :, :]
    var_warped = local_means[2] - local_means[0] * local_means[0]
    var_subject = local_means[3] - local_means[1] * local_means[1]
    covariance = local_means[4] - local_means[0] * local_means[1]
    factor = (centre_subject - local_means[1] - covariance / (var_warped + epsilon) * (centre_warped - local_means[0])) / jnp.sqrt(var_warped * var_subject + epsilon)
    grad_depth = 0.5 * (warped_ext[..., WIN + 1:WIN + 1 + length, :, :] - warped_ext[..., WIN - 1:WIN - 1 + length, :, :])
    padded = jnp.pad(centre_warped, [(0, 0)] * (centre_warped.ndim - 2) + [(1, 1), (1, 1)])
    grad_rows = 0.5 * (padded[..., 2:, 1:-1] - padded[..., :-2, 1:-1])
    grad_cols = 0.5 * (padded[..., 1:-1, 2:] - padded[..., 1:-1, :-2])
    return jnp.stack([factor * grad_depth, factor * grad_rows, factor * grad_cols], axis=-4)

def smooth(force_ext, length):
    along = zwindow(force_ext, length, gauss_taps())
    return inplane(along, gauss_matrix(force_ext.shape[-2]), gauss_matrix(force_ext.shape[-1]))

def reference(template, subjects, shifts, fractions):
    depth_len = template.shape[0]
    padded_template = jnp.pad(template.astype(jnp.float32), ((SHIFT, SHIFT + 1), (SHIFT, SHIFT + 1), (SHIFT, SHIFT + 1)))

    def one_subject(carried, inputs):
        image, shift_one, frac_one = inputs
        warped = warp(padded_template, SHIFT, shift_one, frac_one).astype(jnp.float32)
        image_f = image.astype(jnp.float32)
        depth_pad = ((WIN, WIN), (0, 0), (0, 0))
        force = correlation_force(jnp.pad(warped, depth_pad), jnp.pad(image_f, depth_pad), depth_len)
        force_ext = jnp.pad(force, ((0, 0), (SMOOTH, SMOOTH), (0, 0), (0, 0)))
        return (carried + (image_f - warped), smooth(force_ext, depth_len))
    residual, velocity = lax.scan(one_subject, jnp.zeros(template.shape, jnp.float32), (subjects, shifts, fractions))
    return (velocity, residual * (1.0 / math.sqrt(SUBJECTS)))
```

```python
import numpy as np
import jax
import jax.numpy as jnp
from jax import lax
from jax.experimental import pallas as pl
from jax.experimental.pallas import tpu as pltpu
from jax.sharding import PartitionSpec as P

F32=jnp.float32; BF=jnp.bfloat16
SHIFT=2; WIN=4; SM=4; EPS=1e-5
NS=64; HZ=8; EZ=NS+2*HZ; TZ=72; FZ=NS+2*SM

def constants():
    c=np.arange(128)
    d=c[:,None]-c[None,:]
    shift=np.concatenate([(d==k) for k in range(-2,4)],axis=1).astype(np.float32)
    band=(np.abs(d)<=WIN).astype(np.float32)
    diff=0.5*(d==1).astype(np.float32)-0.5*(d==-1).astype(np.float32)
    taps=np.exp(-0.5*np.arange(-4,5,dtype=np.float64)**2/(1.5*1.5)); taps/=taps.sum()
    g=np.where(np.abs(d)<=SM, taps[np.clip(d+4,0,8)],0.0).astype(np.float32)
    tobf=lambda a: a.astype(np.dtype(BF))
    ghi=tobf(g); glo=tobf(g-ghi.astype(np.float32))
    b2=np.concatenate([band,diff],axis=1)
    bb=np.concatenate([band,band],axis=0)
    gg=np.concatenate([ghi,ghi],axis=0)
    return tobf(shift),tobf(b2),tobf(bb),gg,glo,[float(t) for t in taps]

def pick2(x,m4,m2,m1):
    y0=jnp.where(m4,x[4],x[0]); y1=jnp.where(m4,x[5],x[1])
    z0=jnp.where(m2,x[2],y0); z1=jnp.where(m2,x[3],y1); z2=jnp.where(m2,x[4],x[2])
    return jnp.where(m1,z1,z0), jnp.where(m1,z2,z1)

def lane_shift(tpl,shift_ref,TL):
    def step(g,_):
        x=tpl[pl.ds(g*8,8)].astype(F32).reshape(64,128).astype(BF)
        y=jnp.dot(x,shift_ref[...],preferred_element_type=F32)
        for k in range(6):
            TL[k,pl.ds(pl.multiple_of(g*64,64),64),:]=y[:,k*128:(k+1)*128]
        return 0
    lax.fori_loop(0,TZ//8,step,0)

def warp_slice(z,sh,fr,TL):
    rows=lax.broadcasted_iota(jnp.int32,(8,128),0)
    i0=rows+sh[1,z]; i1=i0+1
    fz=fr[0,z].astype(F32); f_r=fr[1,z].astype(F32); fc=fr[2,z].astype(F32)
    w0=jnp.where((i0>=0)&(i0<8),1.0-f_r,0.0); w1=jnp.where((i1>=0)&(i1<8),f_r,0.0)
    i0=i0&7; i1=i1&7
    uc=sh[2,z]; uz=sh[0,z]
    c4=uc==2; c2=(uc==0)|(uc==1); c1=(uc==-1)|(uc==1)
    vals=[]
    for kz in range(6):
        g0=[];g1=[]
        for kc in range(6):
            src=TL[kc,pl.ds(pl.multiple_of((z+kz)*8,8),8),:]
            g0.append(jnp.take_along_axis(src,i0,axis=0)); g1.append(jnp.take_along_axis(src,i1,axis=0))
        a0,b0=pick2(g0,c4,c2,c1); a1,b1=pick2(g1,c4,c2,c1)
        a=w0*a0+w1*a1; b=w0*b0+w1*b1
        vals.append(a+fc*(b-a))
    z4=uz==2; z2=(uz==0)|(uz==1); z1=(uz==-1)|(uz==1)
    p,q=pick2(vals,z4,z2,z1)
    return p+fz*(q-p)

def split_dot(x,bb):
    hi=x.astype(BF); lo=(x-hi.astype(F32)).astype(BF)
    return jnp.dot(jnp.concatenate([hi,lo],axis=1),bb,preferred_element_type=F32)

def lane_J(JT,b2,bb,LW):
    def step(r,_):
        rows=pl.ds(pl.multiple_of(r*EZ,8),EZ)
        J=JT[rows,:]
        LW[1,rows,:]=jnp.dot(J.astype(BF),b2[:,0:128],preferred_element_type=F32)
        LW[3,rows,:]=split_dot(J*J,bb[...])
        return 0
    lax.fori_loop(0,8,step,0)

def lane_I(WT,JT,b2,bb,LW):
    def step(r,_):
        rows=pl.ds(pl.multiple_of(r*EZ,8),EZ)
        J=JT[rows,:]; I=WT[rows,:]
        y=jnp.dot(I.astype(BF),b2[...],preferred_element_type=F32)
        LW[0,rows,:]=y[:,0:128]; LW[5,rows,:]=y[:,128:256]
        LW[2,rows,:]=split_dot(I*I,bb[...])
        LW[4,rows,:]=split_dot(I*J,bb[...])
        return 0
    lax.fori_loop(0,8,step,0)

def row_window(LW,SW,fields):
    def step(g,_):
        for f in fields:
            x=[LW[f,pl.ds(pl.multiple_of(r*EZ+g*8,8),8),:] for r in range(8)]
            p=x[3]+x[4]; A=x[0]+x[1]+x[2]; B=x[5]+x[6]+x[7]
            r0=A+p; r1=r0+x[5]; r2=r1+x[6]; r3=r2+x[7]; r7=p+B; r6=r7+x[2]; r5=r6+x[1]
            for r,v in enumerate([r0,r1,r2,r3,r3,r5,r6,r7]):
                SW[f,pl.ds(g*64+r,8,stride=8),:]=v
        return 0
    lax.fori_loop(0,EZ//8,step,0)

def force_stage(SW,LW,WZ,JZ,FO,lo_edge,hi_edge):
    rows=lax.broadcasted_iota(jnp.int32,(8,128),0)
    inv=1.0/729.0
    def sl(ref,f,zi): return ref[f,pl.ds(pl.multiple_of(zi*8,8),8),:]
    def step(h,_):
        q0=h*8
        S=[]
        for f in range(5):
            x=[sl(SW,f,q0+j) for j in range(16)]
            s2=[x[j]+x[j+1] for j in range(15)]
            s4=[s2[j]+s2[j+2] for j in range(13)]
            S.append([(s4[j]+s4[j+4]+x[j+8])*inv for j in range(8)])
        for j in range(8):
            q=q0+j
            mI,mJ,mII,mJJ,mIJ=[S[f][j] for f in range(5)]
            I=WZ[pl.ds(pl.multiple_of((q+4)*8,8),8),:]; J=JZ[pl.ds(pl.multiple_of((q+4)*8,8),8),:]
            vI=mII-mI*mI; vJ=mJJ-mJ*mJ; cv=mIJ-mI*mJ
            fac=((J-mJ)-cv/(vI+EPS)*(I-mI))*lax.rsqrt(vI*vJ+EPS)
            dead=jnp.logical_or(jnp.logical_and(lo_edge,q<4),jnp.logical_and(hi_edge,q>=NS+4))
            fac=fac*jnp.where(dead,0.0,1.0)
            hf=0.5*fac
            up=WZ[pl.ds(pl.multiple_of((q+5)*8,8),8),:]; dn=WZ[pl.ds(pl.multiple_of((q+3)*8,8),8),:]
            rp=jnp.where(rows==7,0.0,jnp.take_along_axis(I,jnp.minimum(rows+1,7),axis=0))
            rm=jnp.where(rows==0,0.0,jnp.take_along_axis(I,jnp.maximum(rows-1,0),axis=0))
            gc=LW[5,pl.ds(q+4,8,stride=EZ),:]
            qs=pl.ds(pl.multiple_of(q*8,8),8)
            FO[0,qs,:]=hf*(up-dn); FO[1,qs,:]=hf*(rp-rm); FO[2,qs,:]=fac*gc
        return 0
    lax.fori_loop(0,FZ//8,step,0)

def smooth_z(FO,SZ,taps):
    def step(h,_):
        for c in range(3):
            x=[FO[c,pl.ds(pl.multiple_of(h*64+j*8,8),8),:] for j in range(16)]
            for j in range(8):
                y=taps[4]*x[j+4]
                for k in range(1,5): y=y+taps[4+k]*(x[j+4-k]+x[j+4+k])
                SZ[c,pl.ds(h*8+j,8,stride=NS),:]=y
        return 0
    lax.fori_loop(0,NS//8,step,0)

def smooth_rc(SZ,gg,glo,OUT,taps):
    def step(h,_):
        for c in range(3):
            x=[SZ[c,pl.ds(pl.multiple_of(r*NS+h*8,8),8),:] for r in range(8)]
            ys=[]
            for r in range(8):
                y=taps[4]*x[r]
                for k in range(1,5):
                    if r-k>=0 and r+k<8: y=y+taps[4+k]*(x[r-k]+x[r+k])
                    elif r-k>=0: y=y+taps[4+k]*x[r-k]
                    elif r+k<8: y=y+taps[4+k]*x[r+k]
                ys.append(y)
            Y=jnp.concatenate(ys,axis=0)
            hi=Y.astype(BF); lo=(Y-hi.astype(F32)).astype(BF)
            o=jnp.dot(jnp.concatenate([hi,lo],axis=1),gg[...],preferred_element_type=F32)+jnp.dot(hi,glo[...],preferred_element_type=F32)
            for r in range(8):
                OUT[c,pl.ds(h*64+r,8,stride=8),:]=o[r*8:(r+1)*8,:]
        return 0
    lax.fori_loop(0,NS//8,step,0)


MESH = pl.DeviceIdType.MESH
NG = 4
MEMBERS = 64
LOW = 2
HIGH = 3


def remote(src, dst, ssem, rsem, dev):
    return pltpu.make_async_remote_copy(src_ref=src, dst_ref=dst, send_sem=ssem, recv_sem=rsem, device_id=dev, device_id_type=MESH)


def kernel(taps, tmpl, subj_h, sh_h, fr_h, shm, b2, bb, gg, glo, vel, tf,
           tpl, subj, sh, fr, SH, WB, WH, RES, RB, TFB, TL, WT, JT, WZ, JZ, LW, SW, FO, SZ, OUT,
           lsem, tsend, trecv, tlow, thigh, hsend, hrecv, wsend, wrecv, rsend, rrecv, osem):
    gz = lax.axis_index("gz")
    me = lax.axis_index("subj")
    has_lo = gz > 0
    has_hi = gz < NG - 1
    one = lambda b: b.astype(jnp.int32)
    own = tpl.at[pl.ds(LOW + me, 1)]
    c_t = pltpu.make_async_copy(tmpl, own, lsem.at[0])
    c_s = pltpu.make_async_copy(subj_h.at[0], subj, lsem.at[1])
    c_h = pltpu.make_async_copy(sh_h.at[0], sh, lsem.at[2])
    c_f = pltpu.make_async_copy(fr_h.at[0], fr, lsem.at[3])
    for c in (c_t, c_s, c_h, c_f):
        c.start()

    bar = pltpu.get_barrier_semaphore()

    def signal(dev):
        pl.semaphore_signal(bar, inc=1, device_id=dev, device_id_type=MESH)

    def sig(i, _):
        signal((gz, lax.rem(me + i, MEMBERS)))
        return 0
    lax.fori_loop(1, MEMBERS, sig, 0)

    @pl.when(has_lo)
    def _():
        signal((gz - 1, me))
        for k in range(LOW):
            signal((gz - 1, MEMBERS - LOW + k))

    @pl.when(has_hi)
    def _():
        signal((gz + 1, me))
        for k in range(HIGH):
            signal((gz + 1, k))
    sends_up = jnp.logical_and(has_hi, me >= MEMBERS - LOW)
    sends_dn = jnp.logical_and(has_lo, me < HIGH)

    for ref in (WT, JT, WZ, JZ):
        def zero(r, _):
            a = pl.ds(pl.multiple_of(r * EZ, 8), 8)
            b = pl.ds(pl.multiple_of(r * EZ + EZ - 8, 8), 8)
            ref[a, :] = jnp.zeros((8, 128), F32)
            ref[b, :] = jnp.zeros((8, 128), F32)
            return 0
        if ref is WT or ref is JT:
            lax.fori_loop(0, 8, zero, 0)
        else:
            ref[0:64, :] = jnp.zeros((64, 128), F32)
            ref[EZ * 8 - 64:EZ * 8, :] = jnp.zeros((64, 128), F32)

    @pl.when(jnp.logical_not(has_lo))
    def _():
        tpl[0:LOW] = jnp.zeros((LOW, 8, 128), BF)

    @pl.when(jnp.logical_not(has_hi))
    def _():
        tpl[LOW + NS:LOW + NS + HIGH] = jnp.zeros((HIGH, 8, 128), BF)
    tpl[LOW + NS + HIGH:TZ] = jnp.zeros((TZ - LOW - NS - HIGH, 8, 128), BF)

    c_t.wait()
    c_s.wait()
    pl.semaphore_wait(bar, MEMBERS - 1 + one(has_lo) + one(has_hi) + MEMBERS * (one(sends_up) + one(sends_dn)))

    def tsnd(i, _):
        remote(own, own, tsend, trecv, (gz, lax.rem(me + i, MEMBERS))).start()
        return 0
    lax.fori_loop(1, MEMBERS, tsnd, 0)

    @pl.when(sends_up)
    def _():
        def f(i, _):
            remote(own, tpl.at[pl.ds(me - (MEMBERS - LOW), 1)], hsend.at[2], tlow, (gz + 1, i)).start()
            return 0
        lax.fori_loop(0, MEMBERS, f, 0)

    @pl.when(sends_dn)
    def _():
        def f(i, _):
            remote(own, tpl.at[pl.ds(LOW + NS + me, 1)], hsend.at[3], thigh, (gz - 1, i)).start()
            return 0
        lax.fori_loop(0, MEMBERS, f, 0)

    s_dn = remote(subj.at[0:8], SH.at[1], hsend.at[0], hrecv.at[1], (gz - 1, me))
    s_up = remote(subj.at[NS - 8:NS], SH.at[0], hsend.at[1], hrecv.at[0], (gz + 1, me))
    w_dn = remote(WB.at[0], WH.at[1], wsend.at[0], wrecv.at[1], (gz - 1, me))
    w_up = remote(WB.at[1], WH.at[0], wsend.at[1], wrecv.at[0], (gz + 1, me))

    @pl.when(has_lo)
    def _():
        s_dn.start()

    @pl.when(has_hi)
    def _():
        s_up.start()

    def put(T, Z, zi, v):
        T[pl.ds(zi, 8, stride=EZ), :] = v
        Z[pl.ds(pl.multiple_of(zi * 8, 8), 8), :] = v

    def cp(z, _):
        put(JT, JZ, z + 8, subj[z].astype(F32))
        return 0
    lax.fori_loop(0, NS, cp, 0)

    def halos(H, T, Z, sems):
        @pl.when(has_lo)
        def _():
            pltpu.make_async_copy(H.at[0], H.at[0], sems.at[0]).wait()

            def f(i, _):
                put(T, Z, i, H[0, i].astype(F32))
                return 0
            lax.fori_loop(0, 8, f, 0)

        @pl.when(has_hi)
        def _():
            pltpu.make_async_copy(H.at[1], H.at[1], sems.at[1]).wait()

            def f(i, _):
                put(T, Z, NS + 8 + i, H[1, i].astype(F32))
                return 0
            lax.fori_loop(0, 8, f, 0)
    halos(SH, JT, JZ, hrecv)
    lane_J(JT, b2, bb, LW)
    row_window(LW, SW, (1, 3))
    c_h.wait()
    c_f.wait()

    pltpu.make_async_copy(tpl.at[0:MEMBERS - 1], tpl.at[0:MEMBERS - 1], trecv).wait()

    @pl.when(has_lo)
    def _():
        pltpu.make_async_copy(tpl.at[0:LOW], tpl.at[0:LOW], tlow).wait()

    @pl.when(has_hi)
    def _():
        pltpu.make_async_copy(tpl.at[0:HIGH], tpl.at[0:HIGH], thigh).wait()
    lane_shift(tpl, shm, TL)

    def order(i):
        return jnp.where(i < 8, i, jnp.where(i < 16, i + 48, i - 8))

    def rs_send(i):
        z = order(i)

        @pl.when(z != me)
        def _():
            remote(RES.at[z], RB.at[me], rsend, rrecv, (gz, z)).start()

    def wp(i, _):
        z = order(i)
        wb = warp_slice(z, sh, fr, TL).astype(BF)
        w = wb.astype(F32)
        put(WT, WZ, z + 8, w)
        RES[z] = JZ[pl.ds(pl.multiple_of((z + 8) * 8, 8), 8), :] - w

        @pl.when(i < 16)
        def _():
            WB[i // 8, lax.rem(i, 8)] = wb

        @pl.when(i >= 8)
        def _():
            rs_send(i - 8)
        return 0
    lax.fori_loop(0, 18, wp, 0)

    @pl.when(has_lo)
    def _():
        w_dn.start()

    @pl.when(has_hi)
    def _():
        w_up.start()
    lax.fori_loop(18, NS, wp, 0)

    def rs_last(i, _):
        rs_send(i)
        return 0
    lax.fori_loop(NS - 8, NS, rs_last, 0)

    halos(WH, WT, WZ, wrecv)
    lane_I(WT, JT, b2, bb, LW)
    row_window(LW, SW, (0, 2, 4))
    force_stage(SW, LW, WZ, JZ, FO, jnp.logical_not(has_lo), jnp.logical_not(has_hi))
    smooth_z(FO, SZ, taps)
    smooth_rc(SZ, gg, glo, OUT, taps)
    c_o = pltpu.make_async_copy(OUT, vel.at[0], osem.at[0])
    c_o.start()

    pltpu.make_async_copy(RB.at[0:MEMBERS - 1], RB.at[0:MEMBERS - 1], rrecv).wait()

    def add(i, s):
        return s + RB[lax.rem(me + i, MEMBERS)]
    total = lax.fori_loop(1, MEMBERS, add, RES[me])
    TFB[0] = total * (1.0 / 8.0)
    c_tf = pltpu.make_async_copy(TFB, tf, osem.at[1])
    c_tf.start()

    pltpu.make_async_copy(tpl.at[0:MEMBERS - 1], tpl.at[0:MEMBERS - 1], tsend).wait()
    pltpu.make_async_copy(RB.at[0:MEMBERS - 1], RB.at[0:MEMBERS - 1], rsend).wait()

    @pl.when(sends_up)
    def _():
        pltpu.make_async_copy(tpl.at[0:MEMBERS], tpl.at[0:MEMBERS], hsend.at[2]).wait()

    @pl.when(sends_dn)
    def _():
        pltpu.make_async_copy(tpl.at[0:MEMBERS], tpl.at[0:MEMBERS], hsend.at[3]).wait()

    @pl.when(has_lo)
    def _():
        s_dn.wait_send()
        w_dn.wait_send()

    @pl.when(has_hi)
    def _():
        s_up.wait_send()
        w_up.wait_send()
    c_o.wait()
    c_tf.wait()


def per_device(template, subjects, shifts, fractions):
    shiftm, b2m, bbm, ggm, glom, taps = constants()
    V = pltpu.VMEM
    D = pltpu.SemaphoreType.DMA
    any_ = pl.BlockSpec(memory_space=pltpu.HBM)
    vm = pl.BlockSpec(memory_space=pltpu.VMEM)
    import functools
    vel, tf = pl.pallas_call(
        functools.partial(kernel, taps),
        out_shape=(jax.ShapeDtypeStruct((1, 3, 512, 128), F32), jax.ShapeDtypeStruct((1, 8, 128), F32)),
        in_specs=[any_] * 4 + [vm] * 5,
        out_specs=[any_] * 2,
        scratch_shapes=[
            V((TZ, 8, 128), BF), V((64, 8, 128), BF), V((3, 64, 8, 128), jnp.int32), V((3, 64, 8, 128), BF),
            V((2, 8, 8, 128), BF), V((2, 8, 8, 128), BF), V((2, 8, 8, 128), BF),
            V((64, 8, 128), F32), V((64, 8, 128), F32), V((1, 8, 128), F32),
            V((6, TZ * 8, 128), F32), V((640, 128), F32), V((640, 128), F32), V((640, 128), F32), V((640, 128), F32),
            V((6, 640, 128), F32), V((5, 640, 128), F32), V((3, 576, 128), F32), V((3, 512, 128), F32), V((3, 512, 128), F32),
            D((4,)), D(()), D(()), D(()), D(()), D((4,)), D((2,)), D((2,)), D((2,)), D(()), D(()), D((2,)),
        ],
        compiler_params=pltpu.CompilerParams(collective_id=0, has_side_effects=True, vmem_limit_bytes=48 << 20),
    )(template, subjects, shifts, fractions, shiftm, b2m, bbm, ggm, glom)
    return vel.reshape(1, 3, 64, 8, 128), tf


def solution(mesh):
    placed = (
        P(("gz", "subj"), None, None),
        P("subj", "gz", None, None),
        P("subj", None, "gz", None, None),
        P("subj", None, "gz", None, None),
    )
    return jax.shard_map(
        per_device,
        mesh=mesh,
        in_specs=placed,
        out_specs=(P("subj", None, "gz", None, None), P(("gz", "subj"), None, None)),
        check_vma=False,
    )
```

```python
import numpy as np
import jax
import jax.numpy as jnp
from jax import lax
from jax.experimental import pallas as pl
from jax.experimental.pallas import tpu as pltpu
from jax.sharding import PartitionSpec as P

F32=jnp.float32; BF=jnp.bfloat16
SHIFT=2; WIN=4; SM=4; EPS=1e-5
NS=64; HZ=8; EZ=NS+2*HZ; TZ=72; FZ=NS+2*SM

def constants():
    c=np.arange(128)
    d=c[:,None]-c[None,:]
    shift=np.concatenate([(d==k) for k in range(-2,4)],axis=1).astype(np.float32)
    band=(np.abs(d)<=WIN).astype(np.float32)
    diff=0.5*(d==1).astype(np.float32)-0.5*(d==-1).astype(np.float32)
    taps=np.exp(-0.5*np.arange(-4,5,dtype=np.float64)**2/(1.5*1.5)); taps/=taps.sum()
    g=np.where(np.abs(d)<=SM, taps[np.clip(d+4,0,8)],0.0).astype(np.float32)
    tobf=lambda a: a.astype(np.dtype(BF))
    ghi=tobf(g); glo=tobf(g-ghi.astype(np.float32))
    b2=np.concatenate([band,diff],axis=1)
    bb=np.concatenate([band,band],axis=0)
    gg=np.concatenate([ghi,ghi],axis=0)
    return tobf(shift),tobf(b2),tobf(bb),gg,glo,[float(t) for t in taps]

def packed_constants():
    shift,b2,bb,gg,glo,taps=constants()
    return np.concatenate([shift,b2,gg[0:128],glo],axis=1),taps

def pick2(x,m4,m2,m1):
    y0=jnp.where(m4,x[4],x[0]); y1=jnp.where(m4,x[5],x[1])
    z0=jnp.where(m2,x[2],y0); z1=jnp.where(m2,x[3],y1); z2=jnp.where(m2,x[4],x[2])
    return jnp.where(m1,z1,z0), jnp.where(m1,z2,z1)

LG=72
HB=8
UW=4
def lane_shift(tpl,shift_ref,TL):
    def step(g,_):
        x=tpl[pl.ds(g*LG,LG)].astype(F32).reshape(LG*8,128).astype(BF)
        for p in range(3):
            y=jnp.dot(x,shift_ref[:,p*256:(p+1)*256],preferred_element_type=F32)
            for k in range(2):
                TL[2*p+k,pl.ds(pl.multiple_of(g*LG*8,64),LG*8),:]=y[:,k*128:(k+1)*128]
        return 0
    lax.fori_loop(0,TZ//LG,step,0)

def warp_slice(z,sh,fr,TL):
    rows=lax.broadcasted_iota(jnp.int32,(8,128),0)
    i0=rows+sh[1,z]; i1=i0+1
    fz=fr[0,z].astype(F32); f_r=fr[1,z].astype(F32); fc=fr[2,z].astype(F32)
    w0=jnp.where((i0>=0)&(i0<8),1.0-f_r,0.0); w1=jnp.where((i1>=0)&(i1<8),f_r,0.0)
    i0=i0&7; i1=i1&7
    uc=sh[2,z]; uz=sh[0,z]
    c4=uc==2; c2=(uc==0)|(uc==1); c1=(uc==-1)|(uc==1)
    vals=[]
    for kz in range(6):
        g0=[];g1=[]
        for kc in range(6):
            src=TL[kc,pl.ds(pl.multiple_of((z+kz)*8,8),8),:]
            g0.append(jnp.take_along_axis(src,i0,axis=0)); g1.append(jnp.take_along_axis(src,i1,axis=0))
        a0,b0=pick2(g0,c4,c2,c1); a1,b1=pick2(g1,c4,c2,c1)
        a=w0*a0+w1*a1; b=w0*b0+w1*b1
        vals.append(a+fc*(b-a))
    z4=uz==2; z2=(uz==0)|(uz==1); z1=(uz==-1)|(uz==1)
    p,q=pick2(vals,z4,z2,z1)
    return p+fz*(q-p)

def split_dot(x,bb):
    hi=x.astype(BF); lo=(x-hi.astype(F32)).astype(BF)
    return jnp.dot(jnp.concatenate([hi,lo],axis=1),bb,preferred_element_type=F32)

def lane_J(JT,b2,bb,LW):
    def step(r,_):
        rows=pl.ds(pl.multiple_of(r*EZ,8),EZ)
        J=JT[rows,:]
        LW[1,rows,:]=jnp.dot(J.astype(BF),b2[:,0:128],preferred_element_type=F32)
        LW[3,rows,:]=split_dot(J*J,bb[...])
        return 0
    lax.fori_loop(0,8,step,0)

def lane_I(WT,JT,b2,bb,LW):
    def step(r,_):
        rows=pl.ds(pl.multiple_of(r*EZ,8),EZ)
        J=JT[rows,:]; I=WT[rows,:]
        y=jnp.dot(I.astype(BF),b2[...],preferred_element_type=F32)
        LW[0,rows,:]=y[:,0:128]; LW[5,rows,:]=y[:,128:256]
        LW[2,rows,:]=split_dot(I*I,bb[...])
        LW[4,rows,:]=split_dot(I*J,bb[...])
        return 0
    lax.fori_loop(0,8,step,0)

def row_window(LW,SW,fields):
    def step(g,_):
        for f in fields:
            x=[LW[f,pl.ds(pl.multiple_of(r*EZ+g*8,8),8),:] for r in range(8)]
            p=x[3]+x[4]; A=x[0]+x[1]+x[2]; B=x[5]+x[6]+x[7]
            r0=A+p; r1=r0+x[5]; r2=r1+x[6]; r3=r2+x[7]; r7=p+B; r6=r7+x[2]; r5=r6+x[1]
            for r,v in enumerate([r0,r1,r2,r3,r3,r5,r6,r7]):
                SW[f,pl.ds(g*64+r,8,stride=8),:]=v
        return 0
    lax.fori_loop(0,EZ//8,step,0)

def force_stage(SW,LW,WZ,JZ,FO,lo_edge,hi_edge):
    rows=lax.broadcasted_iota(jnp.int32,(8,128),0)
    inv=1.0/729.0
    def sl(ref,f,zi): return ref[f,pl.ds(pl.multiple_of(zi*8,8),8),:]
    def step(h,_):
        q0=h*8
        S=[]
        for f in range(5):
            x=[sl(SW,f,q0+j) for j in range(16)]
            s2=[x[j]+x[j+1] for j in range(15)]
            s4=[s2[j]+s2[j+2] for j in range(13)]
            S.append([(s4[j]+s4[j+4]+x[j+8])*inv for j in range(8)])
        for j in range(8):
            q=q0+j
            mI,mJ,mII,mJJ,mIJ=[S[f][j] for f in range(5)]
            I=WZ[pl.ds(pl.multiple_of((q+4)*8,8),8),:]; J=JZ[pl.ds(pl.multiple_of((q+4)*8,8),8),:]
            vI=mII-mI*mI; vJ=mJJ-mJ*mJ; cv=mIJ-mI*mJ
            fac=((J-mJ)-cv/(vI+EPS)*(I-mI))*lax.rsqrt(vI*vJ+EPS)
            dead=jnp.logical_or(jnp.logical_and(lo_edge,q<4),jnp.logical_and(hi_edge,q>=NS+4))
            fac=fac*jnp.where(dead,0.0,1.0)
            hf=0.5*fac
            up=WZ[pl.ds(pl.multiple_of((q+5)*8,8),8),:]; dn=WZ[pl.ds(pl.multiple_of((q+3)*8,8),8),:]
            rp=jnp.where(rows==7,0.0,jnp.take_along_axis(I,jnp.minimum(rows+1,7),axis=0))
            rm=jnp.where(rows==0,0.0,jnp.take_along_axis(I,jnp.maximum(rows-1,0),axis=0))
            gc=LW[5,pl.ds(q+4,8,stride=EZ),:]
            qs=pl.ds(pl.multiple_of(q*8,8),8)
            FO[0,qs,:]=hf*(up-dn); FO[1,qs,:]=hf*(rp-rm); FO[2,qs,:]=fac*gc
        return 0
    lax.fori_loop(0,FZ//8,step,0)

def smooth_z(FO,SZ,taps):
    def step(h,_):
        for c in range(3):
            x=[FO[c,pl.ds(pl.multiple_of(h*64+j*8,8),8),:] for j in range(16)]
            for j in range(8):
                y=taps[4]*x[j+4]
                for k in range(1,5): y=y+taps[4+k]*(x[j+4-k]+x[j+4+k])
                SZ[c,pl.ds(h*8+j,8,stride=NS),:]=y
        return 0
    lax.fori_loop(0,NS//8,step,0)

def smooth_rc(SZ,gg,glo,OUT,taps):
    def step(t,_):
        c=t//(8//HB); hb=lax.rem(t,8//HB)
        ys=[]
        for hh in range(HB):
            h=hb*HB+hh
            x=[SZ[c,pl.ds(pl.multiple_of(r*NS+h*8,8),8),:] for r in range(8)]
            for r in range(8):
                y=taps[4]*x[r]
                for k in range(1,5):
                    if r-k>=0 and r+k<8: y=y+taps[4+k]*(x[r-k]+x[r+k])
                    elif r-k>=0: y=y+taps[4+k]*x[r-k]
                    elif r+k<8: y=y+taps[4+k]*x[r+k]
                ys.append(y)
        Y=jnp.concatenate(ys,axis=0)
        hi=Y.astype(BF); lo=(Y-hi.astype(F32)).astype(BF)
        o=jnp.dot(jnp.concatenate([hi,lo],axis=1),gg[...],preferred_element_type=F32)+jnp.dot(hi,glo[...],preferred_element_type=F32)
        for hh in range(HB):
            for r in range(8):
                OUT[c,pl.ds((hb*HB+hh)*64+r,8,stride=8),:]=o[hh*64+r*8:hh*64+(r+1)*8,:]
        return 0
    lax.fori_loop(0,3*(8//HB),step,0)


MESH = pl.DeviceIdType.MESH
NG = 4
MEMBERS = 64
LOW = 2
HIGH = 3


def remote(src, dst, ssem, rsem, dev):
    return pltpu.make_async_remote_copy(src_ref=src, dst_ref=dst, send_sem=ssem, recv_sem=rsem, device_id=dev, device_id_type=MESH)


def kernel(taps, tmpl, subj_h, sh_h, fr_h, cst, vel, tf,
           shm, b2, bb, gg, glo, tpl, subj, sh, fr, SH, WB, WH, RES, RB, TFB, TL, WT, JT, WZ, JZ, LW, SW, FO, SZ, OUT,
           csem, lsem, tsend, trecv, tlow, thigh, hsend, hrecv, wsend, wrecv, rsend, rrecv, osem):
    gz = lax.axis_index("gz")
    me = lax.axis_index("subj")
    has_lo = gz > 0
    has_hi = gz < NG - 1
    one = lambda b: b.astype(jnp.int32)
    own = tpl.at[pl.ds(LOW + me, 1)]
    c_t = pltpu.make_async_copy(tmpl, own, lsem.at[0])
    c_s = pltpu.make_async_copy(subj_h.at[0], subj, lsem.at[1])
    c_h = pltpu.make_async_copy(sh_h.at[0], sh, lsem.at[2])
    c_f = pltpu.make_async_copy(fr_h.at[0], fr, lsem.at[3])
    pieces = ((0, 768, shm), (768, 256, b2), (768, 128, bb.at[0:128]), (768, 128, bb.at[128:256]),
              (1024, 128, gg.at[0:128]), (1024, 128, gg.at[128:256]), (1152, 128, glo))
    c_c = [pltpu.make_async_copy(cst.at[:, a:a + n], d, csem.at[i]) for i, (a, n, d) in enumerate(pieces)]
    for c in (c_t, c_s, *c_c[1:4], c_h, c_f, c_c[0], *c_c[4:]):
        c.start()

    bar = pltpu.get_barrier_semaphore()

    def signal(dev):
        pl.semaphore_signal(bar, inc=1, device_id=dev, device_id_type=MESH)

    def sig(i, _):
        signal((gz, lax.rem(me + i, MEMBERS)))
        return 0
    lax.fori_loop(1, MEMBERS, sig, 0)

    @pl.when(has_lo)
    def _():
        signal((gz - 1, me))
        for k in range(LOW):
            signal((gz - 1, MEMBERS - LOW + k))

    @pl.when(has_hi)
    def _():
        signal((gz + 1, me))
        for k in range(HIGH):
            signal((gz + 1, k))
    sends_up = jnp.logical_and(has_hi, me >= MEMBERS - LOW)
    sends_dn = jnp.logical_and(has_lo, me < HIGH)

    for ref in (WT, JT, WZ, JZ):
        def zero(r, _):
            a = pl.ds(pl.multiple_of(r * EZ, 8), 8)
            b = pl.ds(pl.multiple_of(r * EZ + EZ - 8, 8), 8)
            ref[a, :] = jnp.zeros((8, 128), F32)
            ref[b, :] = jnp.zeros((8, 128), F32)
            return 0
        if ref is WT or ref is JT:
            lax.fori_loop(0, 8, zero, 0)
        else:
            ref[0:64, :] = jnp.zeros((64, 128), F32)
            ref[EZ * 8 - 64:EZ * 8, :] = jnp.zeros((64, 128), F32)

    @pl.when(jnp.logical_not(has_lo))
    def _():
        tpl[0:LOW] = jnp.zeros((LOW, 8, 128), BF)

    @pl.when(jnp.logical_not(has_hi))
    def _():
        tpl[LOW + NS:LOW + NS + HIGH] = jnp.zeros((HIGH, 8, 128), BF)
    tpl[LOW + NS + HIGH:TZ] = jnp.zeros((TZ - LOW - NS - HIGH, 8, 128), BF)

    c_t.wait()
    c_s.wait()
    pl.semaphore_wait(bar, MEMBERS - 1 + one(has_lo) + one(has_hi) + MEMBERS * (one(sends_up) + one(sends_dn)))

    def tsnd(i, _):
        remote(own, own, tsend, trecv, (gz, lax.rem(me + i, MEMBERS))).start()
        return 0
    lax.fori_loop(1, MEMBERS, tsnd, 0)

    @pl.when(sends_up)
    def _():
        def f(i, _):
            remote(own, tpl.at[pl.ds(me - (MEMBERS - LOW), 1)], hsend.at[2], tlow, (gz + 1, i)).start()
            return 0
        lax.fori_loop(0, MEMBERS, f, 0)

    @pl.when(sends_dn)
    def _():
        def f(i, _):
            remote(own, tpl.at[pl.ds(LOW + NS + me, 1)], hsend.at[3], thigh, (gz - 1, i)).start()
            return 0
        lax.fori_loop(0, MEMBERS, f, 0)

    s_dn = remote(subj.at[0:8], SH.at[1], hsend.at[0], hrecv.at[1], (gz - 1, me))
    s_up = remote(subj.at[NS - 8:NS], SH.at[0], hsend.at[1], hrecv.at[0], (gz + 1, me))
    w_dn = remote(WB.at[0], WH.at[1], wsend.at[0], wrecv.at[1], (gz - 1, me))
    w_up = remote(WB.at[1], WH.at[0], wsend.at[1], wrecv.at[0], (gz + 1, me))

    @pl.when(has_lo)
    def _():
        s_dn.start()

    @pl.when(has_hi)
    def _():
        s_up.start()

    def put(T, Z, zi, v):
        T[pl.ds(zi, 8, stride=EZ), :] = v
        Z[pl.ds(pl.multiple_of(zi * 8, 8), 8), :] = v

    def cp(z, _):
        put(JT, JZ, z + 8, subj[z].astype(F32))
        return 0
    lax.fori_loop(0, NS, cp, 0)

    def halos(H, T, Z, sems):
        @pl.when(has_lo)
        def _():
            pltpu.make_async_copy(H.at[0], H.at[0], sems.at[0]).wait()

            def f(i, _):
                put(T, Z, i, H[0, i].astype(F32))
                return 0
            lax.fori_loop(0, 8, f, 0)

        @pl.when(has_hi)
        def _():
            pltpu.make_async_copy(H.at[1], H.at[1], sems.at[1]).wait()

            def f(i, _):
                put(T, Z, NS + 8 + i, H[1, i].astype(F32))
                return 0
            lax.fori_loop(0, 8, f, 0)
    halos(SH, JT, JZ, hrecv)
    for c in c_c:
        c.wait()
    lane_J(JT, b2, bb, LW)
    row_window(LW, SW, (1, 3))
    c_h.wait()
    c_f.wait()

    pltpu.make_async_copy(tpl.at[0:MEMBERS - 1], tpl.at[0:MEMBERS - 1], trecv).wait()

    @pl.when(has_lo)
    def _():
        pltpu.make_async_copy(tpl.at[0:LOW], tpl.at[0:LOW], tlow).wait()

    @pl.when(has_hi)
    def _():
        pltpu.make_async_copy(tpl.at[0:HIGH], tpl.at[0:HIGH], thigh).wait()
    lane_shift(tpl, shm, TL)

    def order(i):
        return jnp.where(i < 8, i, jnp.where(i < 16, i + 48, i - 8))

    def rs_send(i):
        z = order(i)

        @pl.when(z != me)
        def _():
            remote(RES.at[z], RB.at[me], rsend, rrecv, (gz, z)).start()

    def wp(i, _):
        z = order(i)
        wb = warp_slice(z, sh, fr, TL).astype(BF)
        w = wb.astype(F32)
        put(WT, WZ, z + 8, w)
        RES[z] = JZ[pl.ds(pl.multiple_of((z + 8) * 8, 8), 8), :] - w

        @pl.when(i < 16)
        def _():
            WB[i // 8, lax.rem(i, 8)] = wb

        @pl.when(i >= 8)
        def _():
            rs_send(i - 8)
        return 0
    lax.fori_loop(0, 20, wp, 0, unroll=UW)

    @pl.when(has_lo)
    def _():
        w_dn.start()

    @pl.when(has_hi)
    def _():
        w_up.start()
    lax.fori_loop(20, NS, wp, 0, unroll=UW)

    def rs_last(i, _):
        rs_send(i)
        return 0
    lax.fori_loop(NS - 8, NS, rs_last, 0)

    halos(WH, WT, WZ, wrecv)
    lane_I(WT, JT, b2, bb, LW)
    row_window(LW, SW, (0, 2, 4))
    force_stage(SW, LW, WZ, JZ, FO, jnp.logical_not(has_lo), jnp.logical_not(has_hi))
    smooth_z(FO, SZ, taps)
    smooth_rc(SZ, gg, glo, OUT, taps)
    c_o = pltpu.make_async_copy(OUT, vel.at[0], osem.at[0])
    c_o.start()

    pltpu.make_async_copy(RB.at[0:MEMBERS - 1], RB.at[0:MEMBERS - 1], rrecv).wait()

    def add(i, s):
        return s + RB[lax.rem(me + i, MEMBERS)]
    total = lax.fori_loop(1, MEMBERS, add, RES[me])
    TFB[0] = total * (1.0 / 8.0)
    c_tf = pltpu.make_async_copy(TFB, tf, osem.at[1])
    c_tf.start()

    pltpu.make_async_copy(tpl.at[0:MEMBERS - 1], tpl.at[0:MEMBERS - 1], tsend).wait()
    pltpu.make_async_copy(RB.at[0:MEMBERS - 1], RB.at[0:MEMBERS - 1], rsend).wait()

    @pl.when(sends_up)
    def _():
        pltpu.make_async_copy(tpl.at[0:MEMBERS], tpl.at[0:MEMBERS], hsend.at[2]).wait()

    @pl.when(sends_dn)
    def _():
        pltpu.make_async_copy(tpl.at[0:MEMBERS], tpl.at[0:MEMBERS], hsend.at[3]).wait()

    @pl.when(has_lo)
    def _():
        s_dn.wait_send()
        w_dn.wait_send()

    @pl.when(has_hi)
    def _():
        s_up.wait_send()
        w_up.wait_send()
    c_o.wait()
    c_tf.wait()


def per_device(template, subjects, shifts, fractions):
    cst, taps = packed_constants()
    V = pltpu.VMEM
    D = pltpu.SemaphoreType.DMA
    any_ = pl.BlockSpec(memory_space=pltpu.HBM)
    import functools
    vel, tf = pl.pallas_call(
        functools.partial(kernel, taps),
        out_shape=(jax.ShapeDtypeStruct((1, 3, 512, 128), F32), jax.ShapeDtypeStruct((1, 8, 128), F32)),
        in_specs=[any_] * 5,
        out_specs=[any_] * 2,
        scratch_shapes=[
            V((128, 768), BF), V((128, 256), BF), V((256, 128), BF), V((256, 128), BF), V((128, 128), BF),
            V((TZ, 8, 128), BF), V((64, 8, 128), BF), V((3, 64, 8, 128), jnp.int32), V((3, 64, 8, 128), BF),
            V((2, 8, 8, 128), BF), V((2, 8, 8, 128), BF), V((2, 8, 8, 128), BF),
            V((64, 8, 128), F32), V((64, 8, 128), F32), V((1, 8, 128), F32),
            V((6, TZ * 8, 128), F32), V((640, 128), F32), V((640, 128), F32), V((640, 128), F32), V((640, 128), F32),
            V((6, 640, 128), F32), V((5, 640, 128), F32), V((3, 576, 128), F32), V((3, 512, 128), F32), V((3, 512, 128), F32),
            D((7,)), D((4,)), D(()), D(()), D(()), D(()), D((4,)), D((2,)), D((2,)), D((2,)), D(()), D(()), D((2,)),
        ],
        compiler_params=pltpu.CompilerParams(collective_id=0, has_side_effects=True, vmem_limit_bytes=67043328),
    )(template, subjects, shifts, fractions, cst)
    return vel.reshape(1, 3, 64, 8, 128), tf


def solution(mesh):
    placed = (
        P(("gz", "subj"), None, None),
        P("subj", "gz", None, None),
        P("subj", None, "gz", None, None),
        P("subj", None, "gz", None, None),
    )
    return jax.shard_map(
        per_device,
        mesh=mesh,
        in_specs=placed,
        out_specs=(P("subj", None, "gz", None, None), P(("gz", "subj"), None, None)),
        check_vma=False,
    )
```

```python
import functools

import numpy as np
import jax
import jax.numpy as jnp
from jax import lax
from jax.experimental import pallas as pl
from jax.experimental.pallas import tpu as pltpu
from jax.sharding import PartitionSpec as P

F32=jnp.float32; BF=jnp.bfloat16
SHIFT=2; WIN=4; SM=4; EPS=1e-5
NS=64; HZ=8; EZ=NS+2*HZ; TZ=72; FZ=NS+2*SM

def constants():
    c=np.arange(128)
    d=c[:,None]-c[None,:]
    shift=np.concatenate([(d==k) for k in range(-2,4)],axis=1).astype(np.float32)
    band=(np.abs(d)<=WIN).astype(np.float32)
    diff=0.5*(d==1).astype(np.float32)-0.5*(d==-1).astype(np.float32)
    taps=np.exp(-0.5*np.arange(-4,5,dtype=np.float64)**2/(1.5*1.5)); taps/=taps.sum()
    g=np.where(np.abs(d)<=SM, taps[np.clip(d+4,0,8)],0.0).astype(np.float32)
    tobf=lambda a: a.astype(np.dtype(BF))
    ghi=tobf(g); glo=tobf(g-ghi.astype(np.float32))
    b2=np.concatenate([band,diff],axis=1)
    bb=np.concatenate([band,band],axis=0)
    gg=np.concatenate([ghi,ghi],axis=0)
    return tobf(shift),tobf(b2),tobf(bb),gg,glo,[float(t) for t in taps]

def packed_constants():
    shift,b2,bb,gg,glo,taps=constants()
    return np.concatenate([shift,b2,gg[0:128],glo],axis=1),taps

def pick2(x,m4,m2,m1):
    y0=jnp.where(m4,x[4],x[0]); y1=jnp.where(m4,x[5],x[1])
    z0=jnp.where(m2,x[2],y0); z1=jnp.where(m2,x[3],y1); z2=jnp.where(m2,x[4],x[2])
    return jnp.where(m1,z1,z0), jnp.where(m1,z2,z1)


def lane_shift(tpl,shift_ref,TL,e):
    x=tpl[pl.ds(e*4,4)].astype(F32).reshape(32,128).astype(BF)
    for p in range(3):
        y=jnp.dot(x,shift_ref[:,p*256:(p+1)*256],preferred_element_type=F32)
        for k in range(2):
            TL[2*p+k,pl.ds(pl.multiple_of(e*32,32),32),:]=y[:,k*128:(k+1)*128]

def warp_slice(z,sh,fr,TL):
    rows=lax.broadcasted_iota(jnp.int32,(8,128),0)
    i0=rows+sh[1,z]; i1=i0+1
    fz=fr[0,z].astype(F32); f_r=fr[1,z].astype(F32); fc=fr[2,z].astype(F32)
    w0=jnp.where((i0>=0)&(i0<8),1.0-f_r,0.0); w1=jnp.where((i1>=0)&(i1<8),f_r,0.0)
    i0=i0&7; i1=i1&7
    uc=sh[2,z]; uz=sh[0,z]
    c4=uc==2; c2=(uc==0)|(uc==1); c1=(uc==-1)|(uc==1)
    vals=[]
    for kz in range(6):
        g0=[];g1=[]
        for kc in range(6):
            src=TL[kc,pl.ds(pl.multiple_of((z+kz+2)*8,8),8),:]
            g0.append(jnp.take_along_axis(src,i0,axis=0)); g1.append(jnp.take_along_axis(src,i1,axis=0))
        a0,b0=pick2(g0,c4,c2,c1); a1,b1=pick2(g1,c4,c2,c1)
        a=w0*a0+w1*a1; b=w0*b0+w1*b1
        vals.append(a+fc*(b-a))
    z4=uz==2; z2=(uz==0)|(uz==1); z1=(uz==-1)|(uz==1)
    p,q=pick2(vals,z4,z2,z1)
    return p+fz*(q-p)

def split_dot(x,bb):
    hi=x.astype(BF); lo=(x-hi.astype(F32)).astype(BF)
    return jnp.dot(jnp.concatenate([hi,lo],axis=1),bb,preferred_element_type=F32)

def gather_rows(T,g0,n):
    return jnp.concatenate([T[pl.ds(pl.multiple_of(r*EZ+(g0+g)*8,8),8),:] for g in range(n) for r in range(8)],axis=0)

def put_rows(SW,f,g0,n,y,window):
    for g in range(n):
        x=[y[(g*8+r)*8:(g*8+r+1)*8,:] for r in range(8)]
        if window:
            p=x[3]+x[4]; A=x[0]+x[1]+x[2]; B=x[5]+x[6]+x[7]
            r0=A+p; r1=r0+x[5]; r2=r1+x[6]; r3=r2+x[7]; r7=p+B; r6=r7+x[2]; r5=r6+x[1]
            x=[r0,r1,r2,r3,r3,r5,r6,r7]
        for r in range(8):
            SW[f,pl.ds((g0+g)*64+r,8,stride=8),:]=x[r]

def sums_J(JT,b2,bb,SW,g0,n):
    J=gather_rows(JT,g0,n)
    put_rows(SW,1,g0,n,jnp.dot(J.astype(BF),b2[:,0:128],preferred_element_type=F32),True)
    put_rows(SW,3,g0,n,split_dot(J*J,bb[...]),True)

def sums_I(WT,JT,b2,bb,SW,g0,n):
    J=gather_rows(JT,g0,n); I=gather_rows(WT,g0,n)
    y=jnp.dot(I.astype(BF),b2[...],preferred_element_type=F32)
    put_rows(SW,0,g0,n,y[:,0:128],True)
    put_rows(SW,5,g0,n,y[:,128:256],False)
    put_rows(SW,2,g0,n,split_dot(I*I,bb[...]),True)
    put_rows(SW,4,g0,n,split_dot(I*J,bb[...]),True)

def force_group(SW,WZ,JZ,FO,lo_edge,hi_edge,h):
    rows=lax.broadcasted_iota(jnp.int32,(8,128),0)
    inv=1.0/729.0
    def sl(ref,f,zi): return ref[f,pl.ds(pl.multiple_of(zi*8,8),8),:]
    q0=h*8
    S=[]
    for f in range(5):
        x=[sl(SW,f,q0+j) for j in range(16)]
        s2=[x[j]+x[j+1] for j in range(15)]
        s4=[s2[j]+s2[j+2] for j in range(13)]
        S.append([(s4[j]+s4[j+4]+x[j+8])*inv for j in range(8)])
    for j in range(8):
        q=q0+j
        mI,mJ,mII,mJJ,mIJ=[S[f][j] for f in range(5)]
        I=WZ[pl.ds(pl.multiple_of((q+4)*8,8),8),:]; J=JZ[pl.ds(pl.multiple_of((q+4)*8,8),8),:]
        vI=mII-mI*mI; vJ=mJJ-mJ*mJ; cv=mIJ-mI*mJ
        fac=((J-mJ)-cv/(vI+EPS)*(I-mI))*lax.rsqrt(vI*vJ+EPS)
        dead=jnp.logical_or(jnp.logical_and(lo_edge,q<4),jnp.logical_and(hi_edge,q>=NS+4))
        fac=fac*jnp.where(dead,0.0,1.0)
        hf=0.5*fac
        up=WZ[pl.ds(pl.multiple_of((q+5)*8,8),8),:]; dn=WZ[pl.ds(pl.multiple_of((q+3)*8,8),8),:]
        rp=jnp.where(rows==7,0.0,jnp.take_along_axis(I,jnp.minimum(rows+1,7),axis=0))
        rm=jnp.where(rows==0,0.0,jnp.take_along_axis(I,jnp.maximum(rows-1,0),axis=0))
        gc=sl(SW,5,q+4)
        qs=pl.ds(pl.multiple_of(q*8,8),8)
        FO[0,qs,:]=hf*(up-dn); FO[1,qs,:]=hf*(rp-rm); FO[2,qs,:]=fac*gc

def smooth_z(FO,SZ,taps,h):
    for c in range(3):
        x=[FO[c,pl.ds(pl.multiple_of(h*64+j*8,8),8),:] for j in range(16)]
        for j in range(8):
            y=taps[4]*x[j+4]
            for k in range(1,5): y=y+taps[4+k]*(x[j+4-k]+x[j+4+k])
            SZ[c,pl.ds(h*8+j,8,stride=NS),:]=y

def smooth_rc(SZ,gg,glo,put_out,taps,c,hs):
    ys=[]
    for h in hs:
        x=[SZ[c,pl.ds(pl.multiple_of(r*NS+h*8,8),8),:] for r in range(8)]
        for r in range(8):
            y=taps[4]*x[r]
            for k in range(1,5):
                if r-k>=0 and r+k<8: y=y+taps[4+k]*(x[r-k]+x[r+k])
                elif r-k>=0: y=y+taps[4+k]*x[r-k]
                elif r+k<8: y=y+taps[4+k]*x[r+k]
            ys.append(y)
    Y=jnp.concatenate(ys,axis=0)
    hi=Y.astype(BF); lo=(Y-hi.astype(F32)).astype(BF)
    o=jnp.dot(jnp.concatenate([hi,lo],axis=1),gg[...],preferred_element_type=F32)+jnp.dot(hi,glo[...],preferred_element_type=F32)
    for i,h in enumerate(hs):
        for r in range(8):
            put_out(c,pl.ds(h*64+r,8,stride=8),o[i*64+r*8:i*64+(r+1)*8,:])

def loop(n,f,unroll=1):
    def g(i,_):
        f(i); return 0
    lax.fori_loop(0,n,g,0,unroll=unroll)

def interior(WT,JT,WZ,JZ,b2,bb,gg,glo,SW,FO,SZ,put_out,taps,lo_edge,hi_edge):
    loop(4,lambda i: sums_I(WT,JT,b2,bb,SW,1+2*i,2))
    loop(7,lambda i: force_group(SW,WZ,JZ,FO,lo_edge,hi_edge,1+i))
    loop(6,lambda i: smooth_z(FO,SZ,taps,1+i))
    loop(3,lambda c: smooth_rc(SZ,gg,glo,put_out,taps,c,range(1,7)))

def rim(WT,JT,WZ,JZ,b2,bb,gg,glo,SW,FO,SZ,put_out,taps,lo_edge,hi_edge):
    loop(2,lambda i: sums_I(WT,JT,b2,bb,SW,9*i,1))
    loop(2,lambda i: force_group(SW,WZ,JZ,FO,lo_edge,hi_edge,8*i))
    loop(2,lambda i: smooth_z(FO,SZ,taps,7*i))
    loop(3,lambda c: smooth_rc(SZ,gg,glo,put_out,taps,c,(0,7)))


MESH = pl.DeviceIdType.MESH
NG = 4
MEMBERS = 64
LOW = 2
HIGH = 3
BASE = 4
CH = 16


def remote(src, dst, ssem, rsem, dev):
    return pltpu.make_async_remote_copy(src_ref=src, dst_ref=dst, send_sem=ssem, recv_sem=rsem, device_id=dev, device_id_type=MESH)


def kernel(taps, tmpl, subj_h, sh_h, fr_h, cst, vel, tf,
           shm, b2, bb, gg, glo, tpl, subj, sh, fr, SH, WB, WH, RES, RB, TL, WT, JT, WZ, JZ, SW, FO, SZ,
           csem, lsem, tsend, trecv, tlow, thigh, hsend, hrecv, wsend, wrecv, rsend, rrecv):
    gz = lax.axis_index("gz")
    me = lax.axis_index("subj")
    has_lo = gz > 0
    has_hi = gz < NG - 1
    one = lambda b: b.astype(jnp.int32)
    own = tpl.at[pl.ds(BASE + me, 1)]
    c0 = me // 4
    c_t = pltpu.make_async_copy(tmpl, own, lsem.at[0])
    c_s = pltpu.make_async_copy(subj_h.at[0], subj, lsem.at[1])
    c_h = pltpu.make_async_copy(sh_h.at[0], sh, lsem.at[2])
    c_f = pltpu.make_async_copy(fr_h.at[0], fr, lsem.at[3])
    pieces = ((0, 768, shm), (768, 256, b2), (768, 128, bb.at[0:128]), (768, 128, bb.at[128:256]),
              (1024, 128, gg.at[0:128]), (1024, 128, gg.at[128:256]), (1152, 128, glo))
    c_c = [pltpu.make_async_copy(cst.at[:, a:a + n], d, csem.at[i]) for i, (a, n, d) in enumerate(pieces)]
    for c in (c_t, c_s, *c_c[1:4], c_h, c_f, c_c[0], *c_c[4:]):
        c.start()

    bar = pltpu.get_barrier_semaphore()

    def signal(dev):
        pl.semaphore_signal(bar, inc=1, device_id=dev, device_id_type=MESH)

    def sig(i, _):
        signal((gz, lax.rem(me + i, MEMBERS)))
        return 0
    lax.fori_loop(1, MEMBERS, sig, 0)

    @pl.when(has_lo)
    def _():
        signal((gz - 1, me))
        for k in range(LOW):
            signal((gz - 1, MEMBERS - LOW + k))

    @pl.when(has_hi)
    def _():
        signal((gz + 1, me))
        for k in range(HIGH):
            signal((gz + 1, k))
    sends_up = jnp.logical_and(has_hi, me >= MEMBERS - LOW)
    sends_dn = jnp.logical_and(has_lo, me < HIGH)

    for ref in (WT, JT, WZ, JZ):
        def zero(r, _):
            a = pl.ds(pl.multiple_of(r * EZ, 8), 8)
            b = pl.ds(pl.multiple_of(r * EZ + EZ - 8, 8), 8)
            ref[a, :] = jnp.zeros((8, 128), F32)
            ref[b, :] = jnp.zeros((8, 128), F32)
            return 0
        if ref is WT or ref is JT:
            lax.fori_loop(0, 8, zero, 0)
        else:
            ref[0:64, :] = jnp.zeros((64, 128), F32)
            ref[EZ * 8 - 64:EZ * 8, :] = jnp.zeros((64, 128), F32)

    @pl.when(jnp.logical_not(has_lo))
    def _():
        tpl[BASE - LOW:BASE] = jnp.zeros((LOW, 8, 128), BF)

    @pl.when(jnp.logical_not(has_hi))
    def _():
        tpl[BASE + NS:BASE + NS + HIGH] = jnp.zeros((HIGH, 8, 128), BF)
    tpl[0:BASE - LOW] = jnp.zeros((BASE - LOW, 8, 128), BF)
    tpl[BASE + NS + HIGH:TZ] = jnp.zeros((TZ - BASE - NS - HIGH, 8, 128), BF)

    c_t.wait()
    pl.semaphore_wait(bar, MEMBERS - 1 + one(has_lo) + one(has_hi) + MEMBERS * (one(sends_up) + one(sends_dn)))

    def tsnd(i, _):
        remote(own, own, tsend, trecv.at[c0], (gz, lax.rem(me + i, MEMBERS))).start()
        return 0
    lax.fori_loop(1, MEMBERS, tsnd, 0)

    @pl.when(sends_up)
    def _():
        def f(i, _):
            remote(own, tpl.at[pl.ds(BASE - LOW + me - (MEMBERS - LOW), 1)], hsend.at[2], tlow, (gz + 1, i)).start()
            return 0
        lax.fori_loop(0, MEMBERS, f, 0)

    @pl.when(sends_dn)
    def _():
        def f(i, _):
            remote(own, tpl.at[pl.ds(BASE + NS + me, 1)], hsend.at[3], thigh, (gz - 1, i)).start()
            return 0
        lax.fori_loop(0, MEMBERS, f, 0)

    s_dn = remote(subj.at[0:8], SH.at[1], hsend.at[0], hrecv.at[1], (gz - 1, me))
    s_up = remote(subj.at[NS - 8:NS], SH.at[0], hsend.at[1], hrecv.at[0], (gz + 1, me))
    w_dn = remote(WB.at[0], WH.at[1], wsend.at[0], wrecv.at[1], (gz - 1, me))
    w_up = remote(WB.at[1], WH.at[0], wsend.at[1], wrecv.at[0], (gz + 1, me))

    c_s.wait()

    @pl.when(has_lo)
    def _():
        s_dn.start()

    @pl.when(has_hi)
    def _():
        s_up.start()

    def put(T, Z, zi, v):
        T[pl.ds(zi, 8, stride=EZ), :] = v
        Z[pl.ds(pl.multiple_of(zi * 8, 8), 8), :] = v

    def cp(z, _):
        put(JT, JZ, z + 8, subj[z].astype(F32))
        return 0
    lax.fori_loop(0, NS, cp, 0)

    def halos(H, T, Z, sems):
        @pl.when(has_lo)
        def _():
            pltpu.make_async_copy(H.at[0], H.at[0], sems.at[0]).wait()

            def f(i, _):
                put(T, Z, i, H[0, i].astype(F32))
                return 0
            lax.fori_loop(0, 8, f, 0)

        @pl.when(has_hi)
        def _():
            pltpu.make_async_copy(H.at[1], H.at[1], sems.at[1]).wait()

            def f(i, _):
                put(T, Z, NS + 8 + i, H[1, i].astype(F32))
                return 0
            lax.fori_loop(0, 8, f, 0)
    for c in c_c:
        c.wait()
    loop(4, lambda i: sums_J(JT, b2, bb, SW, 1 + 2 * i, 2))
    c_h.wait()
    c_f.wait()

    def prepare(e):
        in_slab = jnp.logical_and(e >= 0, e < CH)
        ei = jnp.maximum(jnp.minimum(e, CH - 1), 0)

        @pl.when(jnp.logical_and(e < 0, has_lo))
        def _():
            pltpu.make_async_copy(tpl.at[0:LOW], tpl.at[0:LOW], tlow).wait()

        @pl.when(jnp.logical_and(e >= CH, has_hi))
        def _():
            pltpu.make_async_copy(tpl.at[0:HIGH], tpl.at[0:HIGH], thigh).wait()

        @pl.when(e == c0)
        def _():
            pltpu.make_async_copy(tpl.at[0:3], tpl.at[0:3], trecv.at[ei]).wait()

        @pl.when(jnp.logical_and(in_slab, e != c0))
        def _():
            pltpu.make_async_copy(tpl.at[0:4], tpl.at[0:4], trecv.at[ei]).wait()
        lane_shift(tpl, shm, TL, e + 1)

    above, below = CH - 1 - c0, c0
    both = jnp.minimum(above, below)

    def place(k):
        paired = k <= 2 * both
        sign = jnp.where(paired, 2 * lax.rem(k, 2) - 1, jnp.where(above > below, 1, -1))
        return c0 + sign * jnp.where(paired, (k + 1) // 2, k - both), sign

    def after(w):
        for j in range(4):
            z = 4 * w + j

            @pl.when(z != me)
            def _():
                remote(RES.at[z], RB.at[me], rsend, rrecv, (gz, z)).start()

        @pl.when(jnp.logical_and(has_lo, w == jnp.where(c0 == 0, 1, 0)))
        def _():
            w_dn.start()

        @pl.when(jnp.logical_and(has_hi, w == jnp.where(c0 == CH - 1, CH - 2, CH - 1)))
        def _():
            w_up.start()

    def wp(k):
        w, sign = place(k)
        prepare(w + sign)
        for j in range(4):
            z = 4 * w + j
            v = warp_slice(z, sh, fr, TL).astype(BF).astype(F32)
            put(WT, WZ, z + 8, v)
            RES[z] = JZ[pl.ds(pl.multiple_of((z + 8) * 8, 8), 8), :] - v

        def keep(side, at):
            WB[side, pl.ds(at, 4)] = WZ[pl.ds(pl.multiple_of(w * 32 + 64, 32), 32), :].reshape(4, 8, 128).astype(BF)

        @pl.when(w < 2)
        def _():
            keep(0, 4 * w)

        @pl.when(w >= CH - 2)
        def _():
            keep(1, 4 * (w - (CH - 2)))

        @pl.when(k > 0)
        def _():
            after(place(k - 1)[0])

    prepare(c0)
    prepare(c0 + 1)
    loop(CH, wp)
    after(place(CH - 1)[0])

    def put_out(c, rows, v):
        vel[0, c, rows, :] = v
    A = (WT, JT, WZ, JZ, b2, bb, gg, glo, SW, FO, SZ, put_out, taps, jnp.logical_not(has_lo), jnp.logical_not(has_hi))
    interior(*A)
    halos(SH, JT, JZ, hrecv)
    loop(2, lambda i: sums_J(JT, b2, bb, SW, 9 * i, 1))
    halos(WH, WT, WZ, wrecv)
    rim(*A)

    pltpu.make_async_copy(RB.at[0:MEMBERS - 1], RB.at[0:MEMBERS - 1], rrecv).wait()

    def add(i, s):
        return s + RB[lax.rem(me + i, MEMBERS)]
    total = lax.fori_loop(1, MEMBERS, add, RES[me])
    tf[0] = total * (1.0 / 8.0)

    pltpu.make_async_copy(tpl.at[0:MEMBERS - 1], tpl.at[0:MEMBERS - 1], tsend).wait()
    pltpu.make_async_copy(RB.at[0:MEMBERS - 1], RB.at[0:MEMBERS - 1], rsend).wait()

    @pl.when(sends_up)
    def _():
        pltpu.make_async_copy(tpl.at[0:MEMBERS], tpl.at[0:MEMBERS], hsend.at[2]).wait()

    @pl.when(sends_dn)
    def _():
        pltpu.make_async_copy(tpl.at[0:MEMBERS], tpl.at[0:MEMBERS], hsend.at[3]).wait()

    @pl.when(has_lo)
    def _():
        s_dn.wait_send()
        w_dn.wait_send()

    @pl.when(has_hi)
    def _():
        s_up.wait_send()
        w_up.wait_send()


def write_out(a, b, vel, tf, sem):
    copies = [pltpu.make_async_copy(a.at[:, i], vel.at[:, i], sem.at[i]) for i in range(3)]
    copies.append(pltpu.make_async_copy(b, tf, sem.at[3]))
    for c in copies:
        c.start()
    for c in copies:
        c.wait()


def per_device(template, subjects, shifts, fractions):
    cst, taps = packed_constants()
    V = pltpu.VMEM
    D = pltpu.SemaphoreType.DMA
    hbm = pl.BlockSpec(memory_space=pltpu.HBM)
    vm = pl.BlockSpec(memory_space=pltpu.VMEM)
    shapes = (jax.ShapeDtypeStruct((1, 3, 512, 128), F32), jax.ShapeDtypeStruct((1, 8, 128), F32))
    operands = [pltpu.with_memory_space_constraint(a, pltpu.HBM) for a in (template, subjects, shifts, fractions, jnp.asarray(cst))]
    vel, tf = pl.pallas_call(
        functools.partial(kernel, taps),
        out_shape=shapes,
        in_specs=[hbm] * 5,
        out_specs=[vm] * 2,
        scratch_shapes=[
            V((128, 768), BF), V((128, 256), BF), V((256, 128), BF), V((256, 128), BF), V((128, 128), BF),
            V((TZ, 8, 128), BF), V((64, 8, 128), BF), V((3, 64, 8, 128), jnp.int32), V((3, 64, 8, 128), BF),
            V((2, 8, 8, 128), BF), V((2, 8, 8, 128), BF), V((2, 8, 8, 128), BF),
            V((64, 8, 128), F32), V((64, 8, 128), F32),
            V((6, TZ * 8, 128), F32), V((640, 128), F32), V((640, 128), F32), V((640, 128), F32), V((640, 128), F32),
            V((6, 640, 128), F32), V((3, 576, 128), F32), V((3, 512, 128), F32),
            D((7,)), D((4,)), D(()), D((CH,)), D(()), D(()), D((4,)), D((2,)), D((2,)), D((2,)), D(()), D(()),
        ],
        compiler_params=pltpu.CompilerParams(collective_id=0, has_side_effects=True, vmem_limit_bytes=32 << 20),
    )(*operands)
    vel, tf = pl.pallas_call(
        write_out,
        out_shape=shapes,
        in_specs=[vm] * 2,
        out_specs=[hbm] * 2,
        scratch_shapes=[D((4,))],
        compiler_params=pltpu.CompilerParams(vmem_limit_bytes=4 << 20),
    )(vel, tf)
    return vel.reshape(1, 3, 64, 8, 128), tf


def solution(mesh):
    placed = (
        P(("gz", "subj"), None, None),
        P("subj", "gz", None, None),
        P("subj", None, "gz", None, None),
        P("subj", None, "gz", None, None),
    )
    return jax.shard_map(
        per_device,
        mesh=mesh,
        in_specs=placed,
        out_specs=(P("subj", None, "gz", None, None), P(("gz", "subj"), None, None)),
        check_vma=False,
    )
```

```python
import functools

import numpy as np
import jax
import jax.numpy as jnp
from jax import lax
from jax.experimental import pallas as pl
from jax.experimental.pallas import tpu as pltpu
from jax.sharding import PartitionSpec as P

F32=jnp.float32; BF=jnp.bfloat16
SHIFT=2; WIN=4; SM=4; EPS=1e-5
NS=64; HZ=8; EZ=NS+2*HZ; TZ=72; FZ=NS+2*SM

def constants():
    c=np.arange(128)
    d=c[:,None]-c[None,:]
    band=(np.abs(d)<=WIN).astype(np.float32)
    diff=0.5*(d==1).astype(np.float32)-0.5*(d==-1).astype(np.float32)
    taps=np.exp(-0.5*np.arange(-4,5,dtype=np.float64)**2/(1.5*1.5)); taps/=taps.sum()
    g=np.where(np.abs(d)<=SM, taps[np.clip(d+4,0,8)],0.0).astype(np.float32)
    tobf=lambda a: a.astype(np.dtype(BF))
    ghi=tobf(g); glo=tobf(g-ghi.astype(np.float32))
    b2=np.concatenate([band,diff],axis=1)
    bb=np.concatenate([band,band],axis=0)
    gg=np.concatenate([ghi,ghi],axis=0)
    return tobf(b2),tobf(bb),gg,glo,[float(t) for t in taps]

def packed_constants():
    b2,bb,gg,glo,taps=constants()
    return np.concatenate([b2,gg[0:128],glo],axis=1),taps

def pick2(x,m4,m2,m1):
    y0=jnp.where(m4,x[4],x[0]); y1=jnp.where(m4,x[5],x[1])
    z0=jnp.where(m2,x[2],y0); z1=jnp.where(m2,x[3],y1); z2=jnp.where(m2,x[4],x[2])
    return jnp.where(m1,z1,z0), jnp.where(m1,z2,z1)


def lane_shift(tpl,TL,e):
    for j in range(4):
        x=tpl[e*4+j].astype(F32)
        for k in range(6):
            TL[k,pl.ds(pl.multiple_of(e*32+j*8,8),8),:]=x if k==SHIFT else pltpu.roll(x,(SHIFT-k)%128,1)

def warp_slice(z,sh,fr,TL):
    rows=lax.broadcasted_iota(jnp.int32,(8,128),0)
    i0=rows+sh[1,z]; i1=i0+1
    fz=fr[0,z].astype(F32); f_r=fr[1,z].astype(F32); fc=fr[2,z].astype(F32)
    w0=jnp.where((i0>=0)&(i0<8),1.0-f_r,0.0); w1=jnp.where((i1>=0)&(i1<8),f_r,0.0)
    i0=i0&7; i1=i1&7
    uc=sh[2,z]; uz=sh[0,z]
    ic=lax.broadcasted_iota(jnp.int32,(8,128),1)+uc
    v0=jnp.where((ic>=0)&(ic<128),1.0-fc,0.0); v1=jnp.where((ic>=-1)&(ic<127),fc,0.0)
    c4=uc==2; c2=(uc==0)|(uc==1); c1=(uc==-1)|(uc==1)
    vals=[]
    for kz in range(6):
        g0=[];g1=[]
        for kc in range(6):
            src=TL[kc,pl.ds(pl.multiple_of((z+kz+2)*8,8),8),:]
            g0.append(jnp.take_along_axis(src,i0,axis=0)); g1.append(jnp.take_along_axis(src,i1,axis=0))
        a0,b0=pick2(g0,c4,c2,c1); a1,b1=pick2(g1,c4,c2,c1)
        a=w0*a0+w1*a1; b=w0*b0+w1*b1
        vals.append(v0*a+v1*b)
    z4=uz==2; z2=(uz==0)|(uz==1); z1=(uz==-1)|(uz==1)
    p,q=pick2(vals,z4,z2,z1)
    return p+fz*(q-p)

def split_dot(x,bb):
    hi=x.astype(BF); lo=(x-hi.astype(F32)).astype(BF)
    return jnp.dot(jnp.concatenate([hi,lo],axis=1),bb,preferred_element_type=F32)

def gather_rows(T,g0,n):
    return jnp.concatenate([T[pl.ds(pl.multiple_of(r*EZ+(g0+g)*8,8),8),:] for g in range(n) for r in range(8)],axis=0)

def put_rows(SW,f,g0,n,y,window):
    for g in range(n):
        x=[y[(g*8+r)*8:(g*8+r+1)*8,:] for r in range(8)]
        if window:
            p=x[3]+x[4]; A=x[0]+x[1]+x[2]; B=x[5]+x[6]+x[7]
            r0=A+p; r1=r0+x[5]; r2=r1+x[6]; r3=r2+x[7]; r7=p+B; r6=r7+x[2]; r5=r6+x[1]
            x=[r0,r1,r2,r3,r3,r5,r6,r7]
        for r in range(8):
            SW[f,pl.ds((g0+g)*64+r,8,stride=8),:]=x[r]

def sums_J(JT,b2,bb,SW,g0,n):
    J=gather_rows(JT,g0,n)
    put_rows(SW,1,g0,n,jnp.dot(J.astype(BF),b2[:,0:128],preferred_element_type=F32),True)
    put_rows(SW,3,g0,n,split_dot(J*J,bb[...]),True)

def sums_I(WT,JT,b2,bb,SW,g0,n):
    J=gather_rows(JT,g0,n); I=gather_rows(WT,g0,n)
    y=jnp.dot(I.astype(BF),b2[...],preferred_element_type=F32)
    put_rows(SW,0,g0,n,y[:,0:128],True)
    put_rows(SW,5,g0,n,y[:,128:256],False)
    put_rows(SW,2,g0,n,split_dot(I*I,bb[...]),True)
    put_rows(SW,4,g0,n,split_dot(I*J,bb[...]),True)

def force_group(SW,WZ,JZ,FO,lo_edge,hi_edge,h):
    rows=lax.broadcasted_iota(jnp.int32,(8,128),0)
    inv=1.0/729.0
    def sl(ref,f,zi): return ref[f,pl.ds(pl.multiple_of(zi*8,8),8),:]
    q0=h*8
    S=[]
    for f in range(5):
        x=[sl(SW,f,q0+j) for j in range(16)]
        s2=[x[j]+x[j+1] for j in range(15)]
        s4=[s2[j]+s2[j+2] for j in range(13)]
        S.append([(s4[j]+s4[j+4]+x[j+8])*inv for j in range(8)])
    for j in range(8):
        q=q0+j
        mI,mJ,mII,mJJ,mIJ=[S[f][j] for f in range(5)]
        I=WZ[pl.ds(pl.multiple_of((q+4)*8,8),8),:]; J=JZ[pl.ds(pl.multiple_of((q+4)*8,8),8),:]
        vI=mII-mI*mI; vJ=mJJ-mJ*mJ; cv=mIJ-mI*mJ
        fac=((J-mJ)-cv/(vI+EPS)*(I-mI))*lax.rsqrt(vI*vJ+EPS)
        dead=jnp.logical_or(jnp.logical_and(lo_edge,q<4),jnp.logical_and(hi_edge,q>=NS+4))
        fac=fac*jnp.where(dead,0.0,1.0)
        hf=0.5*fac
        up=WZ[pl.ds(pl.multiple_of((q+5)*8,8),8),:]; dn=WZ[pl.ds(pl.multiple_of((q+3)*8,8),8),:]
        rp=jnp.where(rows==7,0.0,jnp.take_along_axis(I,jnp.minimum(rows+1,7),axis=0))
        rm=jnp.where(rows==0,0.0,jnp.take_along_axis(I,jnp.maximum(rows-1,0),axis=0))
        gc=sl(SW,5,q+4)
        qs=pl.ds(pl.multiple_of(q*8,8),8)
        FO[0,qs,:]=hf*(up-dn); FO[1,qs,:]=hf*(rp-rm); FO[2,qs,:]=fac*gc

def smooth_z(FO,SZ,taps,h):
    for c in range(3):
        x=[FO[c,pl.ds(pl.multiple_of(h*64+j*8,8),8),:] for j in range(16)]
        for j in range(8):
            y=taps[4]*x[j+4]
            for k in range(1,5): y=y+taps[4+k]*(x[j+4-k]+x[j+4+k])
            SZ[c,pl.ds(h*8+j,8,stride=NS),:]=y

def smooth_rc(SZ,gg,glo,put_out,taps,c,hs):
    ys=[]
    for h in hs:
        x=[SZ[c,pl.ds(pl.multiple_of(r*NS+h*8,8),8),:] for r in range(8)]
        for r in range(8):
            y=taps[4]*x[r]
            for k in range(1,5):
                if r-k>=0 and r+k<8: y=y+taps[4+k]*(x[r-k]+x[r+k])
                elif r-k>=0: y=y+taps[4+k]*x[r-k]
                elif r+k<8: y=y+taps[4+k]*x[r+k]
            ys.append(y)
    Y=jnp.concatenate(ys,axis=0)
    hi=Y.astype(BF); lo=(Y-hi.astype(F32)).astype(BF)
    o=jnp.dot(jnp.concatenate([hi,lo],axis=1),gg[...],preferred_element_type=F32)+jnp.dot(hi,glo[...],preferred_element_type=F32)
    for i,h in enumerate(hs):
        for r in range(8):
            put_out(c,pl.ds(h*64+r,8,stride=8),o[i*64+r*8:i*64+(r+1)*8,:])

def loop(n,f,unroll=1):
    def g(i,_):
        f(i); return 0
    lax.fori_loop(0,n,g,0,unroll=unroll)

def interior(WT,JT,WZ,JZ,b2,bb,gg,glo,SW,FO,SZ,put_out,taps,lo_edge,hi_edge):
    loop(4,lambda i: sums_I(WT,JT,b2,bb,SW,1+2*i,2))
    loop(7,lambda i: force_group(SW,WZ,JZ,FO,lo_edge,hi_edge,1+i))
    loop(6,lambda i: smooth_z(FO,SZ,taps,1+i))
    loop(3,lambda c: smooth_rc(SZ,gg,glo,put_out,taps,c,range(1,7)))

def rim(WT,JT,WZ,JZ,b2,bb,gg,glo,SW,FO,SZ,put_out,taps,lo_edge,hi_edge):
    loop(2,lambda i: sums_I(WT,JT,b2,bb,SW,9*i,1))
    loop(2,lambda i: force_group(SW,WZ,JZ,FO,lo_edge,hi_edge,8*i))
    loop(2,lambda i: smooth_z(FO,SZ,taps,7*i))
    loop(3,lambda c: smooth_rc(SZ,gg,glo,put_out,taps,c,(0,7)))


MESH = pl.DeviceIdType.MESH
NG = 4
MEMBERS = 64
LOW = 2
HIGH = 3
BASE = 4
CH = 16


def remote(src, dst, ssem, rsem, dev):
    return pltpu.make_async_remote_copy(src_ref=src, dst_ref=dst, send_sem=ssem, recv_sem=rsem, device_id=dev, device_id_type=MESH)


def kernel(taps, tmpl, subj_h, sh_h, fr_h, cst, vel, tf,
           b2, bb, gg, glo, tpl, subj, sh, fr, SH, WB, WH, RES, RB, TL, WT, JT, WZ, JZ, SW, FO, SZ,
           csem, lsem, tsend, trecv, tlow, thigh, hsend, hrecv, wsend, wrecv, rsend, rrecv):
    gz = lax.axis_index("gz")
    me = lax.axis_index("subj")
    has_lo = gz > 0
    has_hi = gz < NG - 1
    one = lambda b: b.astype(jnp.int32)
    own = tpl.at[pl.ds(BASE + me, 1)]
    c0 = me // 4
    c_t = pltpu.make_async_copy(tmpl, own, lsem.at[0])
    c_s = pltpu.make_async_copy(subj_h.at[0], subj, lsem.at[1])
    c_h = pltpu.make_async_copy(sh_h.at[0], sh, lsem.at[2])
    c_f = pltpu.make_async_copy(fr_h.at[0], fr, lsem.at[3])
    pieces = ((0, 256, b2), (0, 128, bb.at[0:128]), (0, 128, bb.at[128:256]),
              (256, 128, gg.at[0:128]), (256, 128, gg.at[128:256]), (384, 128, glo))
    c_c = [pltpu.make_async_copy(cst.at[:, a:a + n], d, csem.at[i]) for i, (a, n, d) in enumerate(pieces)]
    for c in (c_t, c_s, *c_c[0:3], c_h, c_f, *c_c[3:]):
        c.start()

    bar = pltpu.get_barrier_semaphore()

    def signal(dev):
        pl.semaphore_signal(bar, inc=1, device_id=dev, device_id_type=MESH)

    def sig(i, _):
        signal((gz, lax.rem(me + i, MEMBERS)))
        return 0
    lax.fori_loop(1, MEMBERS, sig, 0)

    @pl.when(has_lo)
    def _():
        signal((gz - 1, me))
        for k in range(LOW):
            signal((gz - 1, MEMBERS - LOW + k))

    @pl.when(has_hi)
    def _():
        signal((gz + 1, me))
        for k in range(HIGH):
            signal((gz + 1, k))
    sends_up = jnp.logical_and(has_hi, me >= MEMBERS - LOW)
    sends_dn = jnp.logical_and(has_lo, me < HIGH)

    for ref in (WT, JT, WZ, JZ):
        def zero(r, _):
            a = pl.ds(pl.multiple_of(r * EZ, 8), 8)
            b = pl.ds(pl.multiple_of(r * EZ + EZ - 8, 8), 8)
            ref[a, :] = jnp.zeros((8, 128), F32)
            ref[b, :] = jnp.zeros((8, 128), F32)
            return 0
        if ref is WT or ref is JT:
            lax.fori_loop(0, 8, zero, 0)
        else:
            ref[0:64, :] = jnp.zeros((64, 128), F32)
            ref[EZ * 8 - 64:EZ * 8, :] = jnp.zeros((64, 128), F32)

    @pl.when(jnp.logical_not(has_lo))
    def _():
        tpl[BASE - LOW:BASE] = jnp.zeros((LOW, 8, 128), BF)

    @pl.when(jnp.logical_not(has_hi))
    def _():
        tpl[BASE + NS:BASE + NS + HIGH] = jnp.zeros((HIGH, 8, 128), BF)
    tpl[0:BASE - LOW] = jnp.zeros((BASE - LOW, 8, 128), BF)
    tpl[BASE + NS + HIGH:TZ] = jnp.zeros((TZ - BASE - NS - HIGH, 8, 128), BF)

    c_t.wait()
    pl.semaphore_wait(bar, MEMBERS - 1 + one(has_lo) + one(has_hi) + MEMBERS * (one(sends_up) + one(sends_dn)))

    def tsnd(i, _):
        remote(own, own, tsend, trecv.at[c0], (gz, lax.rem(me + i, MEMBERS))).start()
        return 0
    lax.fori_loop(1, MEMBERS, tsnd, 0)

    @pl.when(sends_up)
    def _():
        def f(i, _):
            remote(own, tpl.at[pl.ds(BASE - LOW + me - (MEMBERS - LOW), 1)], hsend.at[2], tlow, (gz + 1, i)).start()
            return 0
        lax.fori_loop(0, MEMBERS, f, 0)

    @pl.when(sends_dn)
    def _():
        def f(i, _):
            remote(own, tpl.at[pl.ds(BASE + NS + me, 1)], hsend.at[3], thigh, (gz - 1, i)).start()
            return 0
        lax.fori_loop(0, MEMBERS, f, 0)

    s_dn = remote(subj.at[0:8], SH.at[1], hsend.at[0], hrecv.at[1], (gz - 1, me))
    s_up = remote(subj.at[NS - 8:NS], SH.at[0], hsend.at[1], hrecv.at[0], (gz + 1, me))
    w_dn = remote(WB.at[0], WH.at[1], wsend.at[0], wrecv.at[1], (gz - 1, me))
    w_up = remote(WB.at[1], WH.at[0], wsend.at[1], wrecv.at[0], (gz + 1, me))

    c_s.wait()

    @pl.when(has_lo)
    def _():
        s_dn.start()

    @pl.when(has_hi)
    def _():
        s_up.start()

    def put(T, Z, zi, v):
        T[pl.ds(zi, 8, stride=EZ), :] = v
        Z[pl.ds(pl.multiple_of(zi * 8, 8), 8), :] = v

    def cp(z, _):
        put(JT, JZ, z + 8, subj[z].astype(F32))
        return 0
    lax.fori_loop(0, NS, cp, 0)

    def halos(H, T, Z, sems):
        @pl.when(has_lo)
        def _():
            pltpu.make_async_copy(H.at[0], H.at[0], sems.at[0]).wait()

            def f(i, _):
                put(T, Z, i, H[0, i].astype(F32))
                return 0
            lax.fori_loop(0, 8, f, 0)

        @pl.when(has_hi)
        def _():
            pltpu.make_async_copy(H.at[1], H.at[1], sems.at[1]).wait()

            def f(i, _):
                put(T, Z, NS + 8 + i, H[1, i].astype(F32))
                return 0
            lax.fori_loop(0, 8, f, 0)
    for c in c_c:
        c.wait()
    loop(4, lambda i: sums_J(JT, b2, bb, SW, 1 + 2 * i, 2))
    c_h.wait()
    c_f.wait()

    def prepare(e):
        in_slab = jnp.logical_and(e >= 0, e < CH)
        ei = jnp.maximum(jnp.minimum(e, CH - 1), 0)

        @pl.when(jnp.logical_and(e < 0, has_lo))
        def _():
            pltpu.make_async_copy(tpl.at[0:LOW], tpl.at[0:LOW], tlow).wait()

        @pl.when(jnp.logical_and(e >= CH, has_hi))
        def _():
            pltpu.make_async_copy(tpl.at[0:HIGH], tpl.at[0:HIGH], thigh).wait()

        @pl.when(e == c0)
        def _():
            pltpu.make_async_copy(tpl.at[0:3], tpl.at[0:3], trecv.at[ei]).wait()

        @pl.when(jnp.logical_and(in_slab, e != c0))
        def _():
            pltpu.make_async_copy(tpl.at[0:4], tpl.at[0:4], trecv.at[ei]).wait()
        lane_shift(tpl, TL, e + 1)

    s0 = jnp.maximum(jnp.minimum(c0, CH - 2), 1)
    above, below = CH - 2 - s0, s0 - 1
    both = jnp.minimum(above, below)

    def place(k):
        paired = k <= 2 * both
        sign = jnp.where(paired, 2 * lax.rem(k, 2) - 1, jnp.where(above > below, 1, -1))
        w = s0 + sign * jnp.where(paired, (k + 1) // 2, k - both)
        w = jnp.where(k == CH - 2, 0, jnp.where(k == CH - 1, CH - 1, w))
        return w, jnp.where(k == CH - 2, -1, jnp.where(k == CH - 1, 1, sign))

    def after(w):
        for j in range(4):
            z = 4 * w + j

            @pl.when(z != me)
            def _():
                remote(RES.at[z], RB.at[me], rsend, rrecv, (gz, z)).start()

        @pl.when(jnp.logical_and(has_lo, w == 0))
        def _():
            w_dn.start()

        @pl.when(jnp.logical_and(has_hi, w == CH - 1))
        def _():
            w_up.start()

    def wp(k):
        w, sign = place(k)
        prepare(w + sign)
        for j in range(4):
            z = 4 * w + j
            v = warp_slice(z, sh, fr, TL).astype(BF).astype(F32)
            put(WT, WZ, z + 8, v)
            RES[z] = JZ[pl.ds(pl.multiple_of((z + 8) * 8, 8), 8), :] - v

        def keep(side, at):
            WB[side, pl.ds(at, 4)] = WZ[pl.ds(pl.multiple_of(w * 32 + 64, 32), 32), :].reshape(4, 8, 128).astype(BF)

        @pl.when(w < 2)
        def _():
            keep(0, 4 * w)

        @pl.when(w >= CH - 2)
        def _():
            keep(1, 4 * (w - (CH - 2)))

        @pl.when(k > 0)
        def _():
            after(place(k - 1)[0])

    prepare(s0)
    prepare(s0 + 1)
    loop(CH, wp)
    after(place(CH - 1)[0])

    def put_out(c, rows, v):
        vel[0, c, rows, :] = v
    A = (WT, JT, WZ, JZ, b2, bb, gg, glo, SW, FO, SZ, put_out, taps, jnp.logical_not(has_lo), jnp.logical_not(has_hi))
    interior(*A)
    halos(SH, JT, JZ, hrecv)
    loop(2, lambda i: sums_J(JT, b2, bb, SW, 9 * i, 1))
    halos(WH, WT, WZ, wrecv)
    rim(*A)

    pltpu.make_async_copy(RB.at[0:MEMBERS - 1], RB.at[0:MEMBERS - 1], rrecv).wait()

    def add(i, s):
        return s + RB[lax.rem(me + i, MEMBERS)]
    total = lax.fori_loop(1, MEMBERS, add, RES[me])
    tf[0] = total * (1.0 / 8.0)

    pltpu.make_async_copy(tpl.at[0:MEMBERS - 1], tpl.at[0:MEMBERS - 1], tsend).wait()
    pltpu.make_async_copy(RB.at[0:MEMBERS - 1], RB.at[0:MEMBERS - 1], rsend).wait()

    @pl.when(sends_up)
    def _():
        pltpu.make_async_copy(tpl.at[0:MEMBERS], tpl.at[0:MEMBERS], hsend.at[2]).wait()

    @pl.when(sends_dn)
    def _():
        pltpu.make_async_copy(tpl.at[0:MEMBERS], tpl.at[0:MEMBERS], hsend.at[3]).wait()

    @pl.when(has_lo)
    def _():
        s_dn.wait_send()
        w_dn.wait_send()

    @pl.when(has_hi)
    def _():
        s_up.wait_send()
        w_up.wait_send()


def write_out(a, b, vel, tf, sem):
    copies = [pltpu.make_async_copy(a.at[:, i], vel.at[:, i], sem.at[i]) for i in range(3)]
    copies.append(pltpu.make_async_copy(b, tf, sem.at[3]))
    for c in copies:
        c.start()
    for c in copies:
        c.wait()


def per_device(template, subjects, shifts, fractions):
    cst, taps = packed_constants()
    V = pltpu.VMEM
    D = pltpu.SemaphoreType.DMA
    hbm = pl.BlockSpec(memory_space=pltpu.HBM)
    vm = pl.BlockSpec(memory_space=pltpu.VMEM)
    shapes = (jax.ShapeDtypeStruct((1, 3, 512, 128), F32), jax.ShapeDtypeStruct((1, 8, 128), F32))
    operands = [pltpu.with_memory_space_constraint(a, pltpu.HBM) for a in (template, subjects, shifts, fractions, jnp.asarray(cst))]
    vel, tf = pl.pallas_call(
        functools.partial(kernel, taps),
        out_shape=shapes,
        in_specs=[hbm] * 5,
        out_specs=[vm] * 2,
        scratch_shapes=[
            V((128, 256), BF), V((256, 128), BF), V((256, 128), BF), V((128, 128), BF),
            V((TZ, 8, 128), BF), V((64, 8, 128), BF), V((3, 64, 8, 128), jnp.int32), V((3, 64, 8, 128), BF),
            V((2, 8, 8, 128), BF), V((2, 8, 8, 128), BF), V((2, 8, 8, 128), BF),
            V((64, 8, 128), F32), V((64, 8, 128), F32),
            V((6, TZ * 8, 128), F32), V((640, 128), F32), V((640, 128), F32), V((640, 128), F32), V((640, 128), F32),
            V((6, 640, 128), F32), V((3, 576, 128), F32), V((3, 512, 128), F32),
            D((6,)), D((4,)), D(()), D((CH,)), D(()), D(()), D((4,)), D((2,)), D((2,)), D((2,)), D(()), D(()),
        ],
        compiler_params=pltpu.CompilerParams(collective_id=0, has_side_effects=True, vmem_limit_bytes=32 << 20),
    )(*operands)
    vel, tf = pl.pallas_call(
        write_out,
        out_shape=shapes,
        in_specs=[vm] * 2,
        out_specs=[hbm] * 2,
        scratch_shapes=[D((4,))],
        compiler_params=pltpu.CompilerParams(vmem_limit_bytes=4 << 20),
    )(vel, tf)
    return vel.reshape(1, 3, 64, 8, 128), tf


def solution(mesh):
    placed = (
        P(("gz", "subj"), None, None),
        P("subj", "gz", None, None),
        P("subj", None, "gz", None, None),
        P("subj", None, "gz", None, None),
    )
    return jax.shard_map(
        per_device,
        mesh=mesh,
        in_specs=placed,
        out_specs=(P("subj", None, "gz", None, None), P(("gz", "subj"), None, None)),
        check_vma=False,
    )
```

```python
import functools

import numpy as np
import jax
import jax.numpy as jnp
from jax import lax
from jax.experimental import pallas as pl
from jax.experimental.pallas import tpu as pltpu
from jax.sharding import PartitionSpec as P

F32=jnp.float32; BF=jnp.bfloat16
SHIFT=2; WIN=4; SM=4; EPS=1e-5
NS=64; HZ=8; EZ=NS+2*HZ; TZ=72; FZ=NS+2*SM

def constants():
    c=np.arange(128)
    d=c[:,None]-c[None,:]
    band=(np.abs(d)<=WIN).astype(np.float32)
    diff=0.5*(d==1).astype(np.float32)-0.5*(d==-1).astype(np.float32)
    taps=np.exp(-0.5*np.arange(-4,5,dtype=np.float64)**2/(1.5*1.5)); taps/=taps.sum()
    g=np.where(np.abs(d)<=SM, taps[np.clip(d+4,0,8)],0.0).astype(np.float32)
    tobf=lambda a: a.astype(np.dtype(BF))
    ghi=tobf(g); glo=tobf(g-ghi.astype(np.float32))
    b2=np.concatenate([band,diff],axis=1)
    bb=np.concatenate([band,band],axis=0)
    gg=np.concatenate([ghi,ghi],axis=0)
    return tobf(b2),tobf(bb),gg,glo,[float(t) for t in taps]

def packed_constants():
    b2,bb,gg,glo,taps=constants()
    return np.concatenate([b2,gg[0:128],glo],axis=1),taps

def pick2(x,m4,m2,m1):
    y0=jnp.where(m4,x[4],x[0]); y1=jnp.where(m4,x[5],x[1])
    z0=jnp.where(m2,x[2],y0); z1=jnp.where(m2,x[3],y1); z2=jnp.where(m2,x[4],x[2])
    return jnp.where(m1,z1,z0), jnp.where(m1,z2,z1)


def lane_shift(tpl,TL,e,n):
    for j in range(4*n):
        x=tpl[e*4+j].astype(F32)
        for k in range(6):
            TL[k,pl.ds(pl.multiple_of(e*32+j*8,8),8),:]=x if k==SHIFT else pltpu.roll(x,(SHIFT-k)%128,1)

def warp_slice(z,sh,fr,TL):
    rows=lax.broadcasted_iota(jnp.int32,(8,128),0)
    i0=rows+sh[1,z]; i1=i0+1
    fz=fr[0,z].astype(F32); f_r=fr[1,z].astype(F32); fc=fr[2,z].astype(F32)
    w0=jnp.where((i0>=0)&(i0<8),1.0-f_r,0.0); w1=jnp.where((i1>=0)&(i1<8),f_r,0.0)
    i0=i0&7; i1=i1&7
    uc=sh[2,z]; uz=sh[0,z]
    ic=lax.broadcasted_iota(jnp.int32,(8,128),1)+uc
    v0=jnp.where((ic>=0)&(ic<128),1.0-fc,0.0); v1=jnp.where((ic>=-1)&(ic<127),fc,0.0)
    c4=uc==2; c2=(uc==0)|(uc==1); c1=(uc==-1)|(uc==1)
    vals=[]
    for kz in range(6):
        g0=[];g1=[]
        for kc in range(6):
            src=TL[kc,pl.ds(pl.multiple_of((z+kz+2)*8,8),8),:]
            g0.append(jnp.take_along_axis(src,i0,axis=0)); g1.append(jnp.take_along_axis(src,i1,axis=0))
        a0,b0=pick2(g0,c4,c2,c1); a1,b1=pick2(g1,c4,c2,c1)
        a=w0*a0+w1*a1; b=w0*b0+w1*b1
        vals.append(v0*a+v1*b)
    z4=uz==2; z2=(uz==0)|(uz==1); z1=(uz==-1)|(uz==1)
    p,q=pick2(vals,z4,z2,z1)
    return p+fz*(q-p)

def split_dot(x,bb):
    hi=x.astype(BF); lo=(x-hi.astype(F32)).astype(BF)
    return jnp.dot(jnp.concatenate([hi,lo],axis=1),bb,preferred_element_type=F32)

def gather_rows(T,g0,n):
    return jnp.concatenate([T[pl.ds(pl.multiple_of(r*EZ+(g0+g)*8,8),8),:] for g in range(n) for r in range(8)],axis=0)

def put_rows(SW,f,g0,n,y,window):
    for g in range(n):
        x=[y[(g*8+r)*8:(g*8+r+1)*8,:] for r in range(8)]
        if window:
            p=x[3]+x[4]; A=x[0]+x[1]+x[2]; B=x[5]+x[6]+x[7]
            r0=A+p; r1=r0+x[5]; r2=r1+x[6]; r3=r2+x[7]; r7=p+B; r6=r7+x[2]; r5=r6+x[1]
            x=[r0,r1,r2,r3,r3,r5,r6,r7]
        for r in range(8):
            SW[f,pl.ds((g0+g)*64+r,8,stride=8),:]=x[r]

def sums_J(JT,b2,bb,SW,g0,n):
    J=gather_rows(JT,g0,n)
    put_rows(SW,1,g0,n,jnp.dot(J.astype(BF),b2[:,0:128],preferred_element_type=F32),True)
    put_rows(SW,3,g0,n,split_dot(J*J,bb[...]),True)

def sums_I(WT,JT,b2,bb,SW,g0,n):
    J=gather_rows(JT,g0,n); I=gather_rows(WT,g0,n)
    y=jnp.dot(I.astype(BF),b2[...],preferred_element_type=F32)
    put_rows(SW,0,g0,n,y[:,0:128],True)
    put_rows(SW,5,g0,n,y[:,128:256],False)
    put_rows(SW,2,g0,n,split_dot(I*I,bb[...]),True)
    put_rows(SW,4,g0,n,split_dot(I*J,bb[...]),True)

def force_group(SW,WZ,JZ,FO,lo_edge,hi_edge,h):
    rows=lax.broadcasted_iota(jnp.int32,(8,128),0)
    inv=1.0/729.0
    def sl(ref,f,zi): return ref[f,pl.ds(pl.multiple_of(zi*8,8),8),:]
    q0=h*8
    S=[]
    for f in range(5):
        x=[sl(SW,f,q0+j) for j in range(16)]
        s2=[x[j]+x[j+1] for j in range(15)]
        s4=[s2[j]+s2[j+2] for j in range(13)]
        S.append([(s4[j]+s4[j+4]+x[j+8])*inv for j in range(8)])
    for j in range(8):
        q=q0+j
        mI,mJ,mII,mJJ,mIJ=[S[f][j] for f in range(5)]
        I=WZ[pl.ds(pl.multiple_of((q+4)*8,8),8),:]; J=JZ[pl.ds(pl.multiple_of((q+4)*8,8),8),:]
        vI=mII-mI*mI; vJ=mJJ-mJ*mJ; cv=mIJ-mI*mJ
        fac=((J-mJ)-cv/(vI+EPS)*(I-mI))*lax.rsqrt(vI*vJ+EPS)
        dead=jnp.logical_or(jnp.logical_and(lo_edge,q<4),jnp.logical_and(hi_edge,q>=NS+4))
        fac=fac*jnp.where(dead,0.0,1.0)
        hf=0.5*fac
        up=WZ[pl.ds(pl.multiple_of((q+5)*8,8),8),:]; dn=WZ[pl.ds(pl.multiple_of((q+3)*8,8),8),:]
        rp=jnp.where(rows==7,0.0,jnp.take_along_axis(I,jnp.minimum(rows+1,7),axis=0))
        rm=jnp.where(rows==0,0.0,jnp.take_along_axis(I,jnp.maximum(rows-1,0),axis=0))
        gc=sl(SW,5,q+4)
        qs=pl.ds(pl.multiple_of(q*8,8),8)
        FO[0,qs,:]=hf*(up-dn); FO[1,qs,:]=hf*(rp-rm); FO[2,qs,:]=fac*gc

def smooth_z(FO,SZ,taps,h):
    for c in range(3):
        x=[FO[c,pl.ds(pl.multiple_of(h*64+j*8,8),8),:] for j in range(16)]
        for j in range(8):
            y=taps[4]*x[j+4]
            for k in range(1,5): y=y+taps[4+k]*(x[j+4-k]+x[j+4+k])
            SZ[c,pl.ds(h*8+j,8,stride=NS),:]=y

def smooth_rc(SZ,gg,glo,put_out,taps,c,hs):
    ys=[]
    for h in hs:
        x=[SZ[c,pl.ds(pl.multiple_of(r*NS+h*8,8),8),:] for r in range(8)]
        for r in range(8):
            y=taps[4]*x[r]
            for k in range(1,5):
                if r-k>=0 and r+k<8: y=y+taps[4+k]*(x[r-k]+x[r+k])
                elif r-k>=0: y=y+taps[4+k]*x[r-k]
                elif r+k<8: y=y+taps[4+k]*x[r+k]
            ys.append(y)
    Y=jnp.concatenate(ys,axis=0)
    hi=Y.astype(BF); lo=(Y-hi.astype(F32)).astype(BF)
    o=jnp.dot(jnp.concatenate([hi,lo],axis=1),gg[...],preferred_element_type=F32)+jnp.dot(hi,glo[...],preferred_element_type=F32)
    for i,h in enumerate(hs):
        for r in range(8):
            put_out(c,pl.ds(h*64+r,8,stride=8),o[i*64+r*8:i*64+(r+1)*8,:])

def loop(n,f,unroll=1):
    def g(i,_):
        f(i); return 0
    lax.fori_loop(0,n,g,0,unroll=unroll)

def interior(WT,JT,WZ,JZ,b2,bb,gg,glo,SW,FO,SZ,put_out,taps,lo_edge,hi_edge):
    loop(4,lambda i: sums_I(WT,JT,b2,bb,SW,1+2*i,2))
    loop(7,lambda i: force_group(SW,WZ,JZ,FO,lo_edge,hi_edge,1+i))
    loop(6,lambda i: smooth_z(FO,SZ,taps,1+i))
    loop(3,lambda c: smooth_rc(SZ,gg,glo,put_out,taps,c,range(1,7)))

def rim(WT,JT,WZ,JZ,b2,bb,gg,glo,SW,FO,SZ,put_out,taps,lo_edge,hi_edge):
    loop(2,lambda i: sums_I(WT,JT,b2,bb,SW,9*i,1))
    loop(2,lambda i: force_group(SW,WZ,JZ,FO,lo_edge,hi_edge,8*i))
    loop(2,lambda i: smooth_z(FO,SZ,taps,7*i))
    loop(3,lambda c: smooth_rc(SZ,gg,glo,put_out,taps,c,(0,7)))


MESH = pl.DeviceIdType.MESH
NG = 4
MEMBERS = 64
LOW = 2
HIGH = 3
BASE = 4
CH = 16
FAR = (2, 3, 1, 0)


def remote(src, dst, ssem, rsem, dev):
    return pltpu.make_async_remote_copy(src_ref=src, dst_ref=dst, send_sem=ssem, recv_sem=rsem, device_id=dev, device_id_type=MESH)


def kernel(taps, tmpl, subj_h, sh_h, fr_h, cst, vel, tf,
           b2, bb, gg, glo, tpl, subj, sh, fr, SH, WH, WBF, RBJ, RBW, TL, WT, JT, WZ, JZ, SW, FO, SZ,
           csem, lsem, tsend, trecv, tlow, thigh, hsend, hrecv, wsend, wrecv, rsend, rrecv, jsend, jrecv, xs):
    gz = lax.axis_index("gz")
    me = lax.axis_index("subj")
    has_lo = gz > 0
    has_hi = gz < NG - 1
    one = lambda b: b.astype(jnp.int32)
    own = tpl.at[pl.ds(BASE + me, 1)]
    c0 = me // 4
    c_t = pltpu.make_async_copy(tmpl, own, lsem.at[0])
    c_s = pltpu.make_async_copy(subj_h.at[0], subj, lsem.at[1])
    c_h = pltpu.make_async_copy(sh_h.at[0], sh, lsem.at[2])
    c_f = pltpu.make_async_copy(fr_h.at[0], fr, lsem.at[3])
    pieces = ((0, 256, b2), (0, 128, bb.at[0:128]), (0, 128, bb.at[128:256]),
              (256, 128, gg.at[0:128]), (256, 128, gg.at[128:256]), (384, 128, glo))
    c_c = [pltpu.make_async_copy(cst.at[:, a:a + n], d, csem.at[i]) for i, (a, n, d) in enumerate(pieces)]
    for c in (c_t, c_s, *c_c[0:3], c_h, c_f, *c_c[3:]):
        c.start()

    bar = pltpu.get_barrier_semaphore()

    def signal(dev):
        pl.semaphore_signal(bar, inc=1, device_id=dev, device_id_type=MESH)

    px, pz, py = me // 16, lax.rem(me // 4, 4), lax.rem(me, 4)
    at_x = [lax.rem(px + d, 4) * 16 for d in range(4)]
    at_z = [lax.rem(pz + d, 4) * 4 for d in range(4)]
    at_y = [lax.rem(py + d, 4) for d in range(4)]
    peers = [at_x[a] + at_z[b] + at_y[d] for a in FAR for b in FAR for d in FAR if a + b + d > 0]
    for p in peers:
        signal((gz, p))

    @pl.when(has_lo)
    def _():
        for k in range(LOW):
            signal((gz - 1, MEMBERS - LOW + k))

    @pl.when(has_hi)
    def _():
        signal((gz + 1, me))
        for k in range(HIGH):
            signal((gz + 1, k))
    sends_up = jnp.logical_and(has_hi, me >= MEMBERS - LOW)
    sends_dn = jnp.logical_and(has_lo, me < HIGH)

    for ref in (WT, JT, WZ, JZ):
        def zero(r, _):
            a = pl.ds(pl.multiple_of(r * EZ, 8), 8)
            b = pl.ds(pl.multiple_of(r * EZ + EZ - 8, 8), 8)
            ref[a, :] = jnp.zeros((8, 128), F32)
            ref[b, :] = jnp.zeros((8, 128), F32)
            return 0
        if ref is WT or ref is JT:
            lax.fori_loop(0, 8, zero, 0)
        else:
            ref[0:64, :] = jnp.zeros((64, 128), F32)
            ref[EZ * 8 - 64:EZ * 8, :] = jnp.zeros((64, 128), F32)

    @pl.when(jnp.logical_not(has_lo))
    def _():
        tpl[BASE - LOW:BASE] = jnp.zeros((LOW, 8, 128), BF)

    @pl.when(jnp.logical_not(has_hi))
    def _():
        tpl[BASE + NS:BASE + NS + HIGH] = jnp.zeros((HIGH, 8, 128), BF)
    tpl[0:BASE - LOW] = jnp.zeros((BASE - LOW, 8, 128), BF)
    tpl[BASE + NS + HIGH:TZ] = jnp.zeros((TZ - BASE - NS - HIGH, 8, 128), BF)

    def put(T, Z, zi, v):
        T[pl.ds(zi, 8, stride=EZ), :] = v
        Z[pl.ds(pl.multiple_of(zi * 8, 8), 8), :] = v

    def subject_sums():
        loop(NS, lambda z: put(JT, JZ, z + 8, subj[z].astype(F32)), unroll=4)
        for c in c_c:
            c.wait()
        loop(4, lambda i: sums_J(JT, b2, bb, SW, 1 + 2 * i, 2))
    dist = jnp.minimum(px, 4 - px) + jnp.minimum(py, 4 - py) + jnp.where(gz < 2, pz, 4 - pz)
    early = dist < 4

    @pl.when(early)
    def _():
        c_s.wait()
        subject_sums()

    c_t.wait()
    pl.semaphore_wait(bar, MEMBERS - 1 + one(has_lo) + MEMBERS * (one(sends_up) + one(sends_dn)))

    @pl.when(sends_up)
    def _():
        def f(i, _):
            remote(own, tpl.at[pl.ds(BASE - LOW + me - (MEMBERS - LOW), 1)], hsend.at[2], tlow, (gz + 1, i)).start()
            return 0
        lax.fori_loop(0, MEMBERS, f, 0)

    @pl.when(sends_dn)
    def _():
        def f(i, _):
            remote(own, tpl.at[pl.ds(BASE + NS + me, 1)], hsend.at[3], thigh, (gz - 1, i)).start()
            return 0
        lax.fori_loop(0, MEMBERS, f, 0)

    for p in peers:
        remote(own, own, tsend, trecv.at[c0], (gz, p)).start()

    s_dn = remote(subj.at[0:8], SH.at[1], hsend.at[0], hrecv.at[1], (gz - 1, me))
    s_up = remote(subj.at[NS - 8:NS], SH.at[0], hsend.at[1], hrecv.at[0], (gz + 1, me))
    w_dn = remote(WBF.at[0:8], WH.at[1], wsend.at[0], wrecv.at[1], (gz - 1, me))
    w_up = remote(WBF.at[NS - 8:NS], WH.at[0], wsend.at[1], wrecv.at[0], (gz + 1, me))


    @pl.when(has_lo)
    def _():
        pl.semaphore_signal(xs, inc=1, device_id=(gz - 1, me), device_id_type=MESH)
    @pl.when(jnp.logical_not(early))
    def _():
        c_s.wait()

    @pl.when(has_lo)
    def _():
        s_dn.start()

    for p in peers:
        remote(subj.at[p], RBJ.at[me], jsend, jrecv, (gz, p)).start()

    def halos(H, T, Z, sems):
        @pl.when(has_lo)
        def _():
            pltpu.make_async_copy(H.at[0], H.at[0], sems.at[0]).wait()

            def f(i, _):
                put(T, Z, i, H[0, i].astype(F32))
                return 0
            lax.fori_loop(0, 8, f, 0)

        @pl.when(has_hi)
        def _():
            pltpu.make_async_copy(H.at[1], H.at[1], sems.at[1]).wait()

            def f(i, _):
                put(T, Z, NS + 8 + i, H[1, i].astype(F32))
                return 0
            lax.fori_loop(0, 8, f, 0)
    c_h.wait()
    c_f.wait()

    def prepare(e):
        in_slab = jnp.logical_and(e >= 0, e < CH)
        ei = jnp.maximum(jnp.minimum(e, CH - 1), 0)

        @pl.when(jnp.logical_and(e < 0, has_lo))
        def _():
            pltpu.make_async_copy(tpl.at[0:LOW], tpl.at[0:LOW], tlow).wait()

        @pl.when(jnp.logical_and(e >= CH, has_hi))
        def _():
            pltpu.make_async_copy(tpl.at[0:HIGH], tpl.at[0:HIGH], thigh).wait()

        @pl.when(e == c0)
        def _():
            pltpu.make_async_copy(tpl.at[0:3], tpl.at[0:3], trecv.at[ei]).wait()

        @pl.when(jnp.logical_and(in_slab, e != c0))
        def _():
            pltpu.make_async_copy(tpl.at[0:4], tpl.at[0:4], trecv.at[ei]).wait()
        lane_shift(tpl, TL, e + 1, 1)

    rising = gz == 2
    s0 = jnp.maximum(jnp.minimum(c0, CH - 2), 1)
    above, below = CH - 2 - s0, s0 - 1
    both = jnp.minimum(above, below)

    def place(k):
        paired = k <= 2 * both
        sign = jnp.where(paired, 2 * lax.rem(k, 2) - 1, jnp.where(above > below, 1, -1))
        w = s0 + sign * jnp.where(paired, (k + 1) // 2, k - both)
        w = jnp.where(k == CH - 2, 0, jnp.where(k == CH - 1, CH - 1, w))
        sign = jnp.where(k == CH - 2, -1, jnp.where(k == CH - 1, 1, sign))
        return jnp.where(rising, k, w), jnp.where(rising, 1, sign)

    beside = lax.rem(me + 1, MEMBERS)

    def after(w):
        for j in range(4):
            z = 4 * w + j
            mine = z == me
            to = jnp.where(mine, beside, z)
            remote(WBF.at[z], RBW.at[jnp.where(mine, MEMBERS, me)], rsend, rrecv, (gz, to)).start()

        @pl.when(jnp.logical_and(has_lo, w == jnp.where(rising, 1, 0)))
        def _():
            w_dn.start()

        @pl.when(jnp.logical_and(has_hi, w == CH - 1))
        def _():
            w_up.start()

    def wp(k):
        w, sign = place(k)
        prepare(w + sign)
        for j in range(4):
            z = 4 * w + j
            v = warp_slice(z, sh, fr, TL).astype(BF)
            WBF[z] = v
            put(WT, WZ, z + 8, v.astype(F32))

        @pl.when(k > 0)
        def _():
            after(place(k - 1)[0])

    first = jnp.where(rising, 0, s0)
    prepare(first)
    prepare(first + jnp.where(rising, -1, 1))
    loop(CH - 1, wp)

    @pl.when(has_hi)
    def _():
        pl.semaphore_wait(xs, 1)
        s_up.start()
    wp(CH - 1)
    after(place(CH - 1)[0])

    @pl.when(jnp.logical_not(early))
    def _():
        subject_sums()

    RBW[me] = WBF[me]
    RBJ[me] = subj[me]

    def put_out(c, rows, v):
        vel[0, c, rows, :] = v
    A = (WT, JT, WZ, JZ, b2, bb, gg, glo, SW, FO, SZ, put_out, taps, jnp.logical_not(has_lo), jnp.logical_not(has_hi))
    interior(*A)
    halos(SH, JT, JZ, hrecv)
    loop(2, lambda i: sums_J(JT, b2, bb, SW, 9 * i, 1))
    halos(WH, WT, WZ, wrecv)
    rim(*A)

    def total(R, n, sem):
        pltpu.make_async_copy(R.at[0:n], R.at[0:n], sem).wait()
        parts = [R[i].astype(F32) for i in range(MEMBERS)]
        while len(parts) > 1:
            parts = [a + b for a, b in zip(parts[0::2], parts[1::2])]
        return parts[0]
    tf[0] = (total(RBJ, MEMBERS - 1, jrecv) - total(RBW, MEMBERS, rrecv)) * (1.0 / 8.0)

    pltpu.make_async_copy(tpl.at[0:MEMBERS - 1], tpl.at[0:MEMBERS - 1], tsend).wait()
    pltpu.make_async_copy(RBW.at[0:MEMBERS], RBW.at[0:MEMBERS], rsend).wait()
    pltpu.make_async_copy(RBJ.at[0:MEMBERS - 1], RBJ.at[0:MEMBERS - 1], jsend).wait()

    @pl.when(sends_up)
    def _():
        pltpu.make_async_copy(tpl.at[0:MEMBERS], tpl.at[0:MEMBERS], hsend.at[2]).wait()

    @pl.when(sends_dn)
    def _():
        pltpu.make_async_copy(tpl.at[0:MEMBERS], tpl.at[0:MEMBERS], hsend.at[3]).wait()

    @pl.when(has_lo)
    def _():
        s_dn.wait_send()
        w_dn.wait_send()

    @pl.when(has_hi)
    def _():
        s_up.wait_send()
        w_up.wait_send()


def write_out(a, b, vel, tf, sem):
    copies = [pltpu.make_async_copy(a.at[:, i], vel.at[:, i], sem.at[i]) for i in range(3)]
    copies.append(pltpu.make_async_copy(b, tf, sem.at[3]))
    for c in copies:
        c.start()
    for c in copies:
        c.wait()


def per_device(template, subjects, shifts, fractions):
    cst, taps = packed_constants()
    V = pltpu.VMEM
    D = pltpu.SemaphoreType.DMA
    hbm = pl.BlockSpec(memory_space=pltpu.HBM)
    vm = pl.BlockSpec(memory_space=pltpu.VMEM)
    shapes = (jax.ShapeDtypeStruct((1, 3, 512, 128), F32), jax.ShapeDtypeStruct((1, 8, 128), F32))
    operands = [pltpu.with_memory_space_constraint(a, pltpu.HBM) for a in (template, subjects, shifts, fractions, jnp.asarray(cst))]
    vel, tf = pl.pallas_call(
        functools.partial(kernel, taps),
        out_shape=shapes,
        in_specs=[hbm] * 5,
        out_specs=[vm] * 2,
        scratch_shapes=[
            V((128, 256), BF), V((256, 128), BF), V((256, 128), BF), V((128, 128), BF),
            V((TZ, 8, 128), BF), V((64, 8, 128), BF), V((3, 64, 8, 128), jnp.int32), V((3, 64, 8, 128), BF),
            V((2, 8, 8, 128), BF), V((2, 8, 8, 128), BF),
            V((64, 8, 128), BF), V((64, 8, 128), BF), V((65, 8, 128), BF),
            V((6, TZ * 8, 128), F32), V((640, 128), F32), V((640, 128), F32), V((640, 128), F32), V((640, 128), F32),
            V((6, 640, 128), F32), V((3, 576, 128), F32), V((3, 512, 128), F32),
            D((6,)), D((4,)), D(()), D((CH,)), D(()), D(()), D((4,)), D((2,)), D((2,)), D((2,)), D(()), D(()), D(()), D(()), pltpu.SemaphoreType.REGULAR,
        ],
        compiler_params=pltpu.CompilerParams(collective_id=0, has_side_effects=True, vmem_limit_bytes=32 << 20),
    )(*operands)
    vel, tf = pl.pallas_call(
        write_out,
        out_shape=shapes,
        in_specs=[vm] * 2,
        out_specs=[hbm] * 2,
        scratch_shapes=[D((4,))],
        compiler_params=pltpu.CompilerParams(vmem_limit_bytes=4 << 20),
    )(vel, tf)
    return vel.reshape(1, 3, 64, 8, 128), tf


def solution(mesh):
    placed = (
        P(("gz", "subj"), None, None),
        P("subj", "gz", None, None),
        P("subj", None, "gz", None, None),
        P("subj", None, "gz", None, None),
    )
    return jax.shard_map(
        per_device,
        mesh=mesh,
        in_specs=placed,
        out_specs=(P("subj", None, "gz", None, None), P(("gz", "subj"), None, None)),
        check_vma=False,
    )
```

```python
import functools

import numpy as np
import jax
import jax.numpy as jnp
from jax import lax
from jax.experimental import pallas as pl
from jax.experimental.pallas import tpu as pltpu
from jax.sharding import PartitionSpec as P

F32=jnp.float32; BF=jnp.bfloat16
SHIFT=2; WIN=4; SM=4; EPS=1e-5
NS=64; HZ=8; EZ=NS+2*HZ; TZ=72; FZ=NS+2*SM

def constants():
    c=np.arange(128)
    d=c[:,None]-c[None,:]
    band=(np.abs(d)<=WIN).astype(np.float32)
    diff=0.5*(d==1).astype(np.float32)-0.5*(d==-1).astype(np.float32)
    taps=np.exp(-0.5*np.arange(-4,5,dtype=np.float64)**2/(1.5*1.5)); taps/=taps.sum()
    g=np.where(np.abs(d)<=SM, taps[np.clip(d+4,0,8)],0.0).astype(np.float32)
    tobf=lambda a: a.astype(np.dtype(BF))
    ghi=tobf(g); glo=tobf(g-ghi.astype(np.float32))
    b2=np.concatenate([band,diff],axis=1)
    bb=np.concatenate([band,band],axis=0)
    gg=np.concatenate([ghi,ghi],axis=0)
    return tobf(b2),tobf(bb),gg,glo,[float(t) for t in taps]

def packed_constants():
    b2,bb,gg,glo,taps=constants()
    return np.concatenate([b2,gg[0:128],glo],axis=1),taps

def pick2(x,m4,m2,m1):
    y0=jnp.where(m4,x[4],x[0]); y1=jnp.where(m4,x[5],x[1])
    z0=jnp.where(m2,x[2],y0); z1=jnp.where(m2,x[3],y1); z2=jnp.where(m2,x[4],x[2])
    return jnp.where(m1,z1,z0), jnp.where(m1,z2,z1)


def lane_shift(tpl,TL,e,n):
    for j in range(4*n):
        x=tpl[e*4+j].astype(F32)
        for k in range(6):
            TL[k,pl.ds(pl.multiple_of(e*32+j*8,8),8),:]=x if k==SHIFT else pltpu.roll(x,(SHIFT-k)%128,1)

def warp_slice(z,sh,fr,TL):
    rows=lax.broadcasted_iota(jnp.int32,(8,128),0)
    i0=rows+sh[1,z]; i1=i0+1
    fz=fr[0,z].astype(F32); f_r=fr[1,z].astype(F32); fc=fr[2,z].astype(F32)
    w0=jnp.where((i0>=0)&(i0<8),1.0-f_r,0.0); w1=jnp.where((i1>=0)&(i1<8),f_r,0.0)
    i0=i0&7; i1=i1&7
    uc=sh[2,z]; uz=sh[0,z]
    ic=lax.broadcasted_iota(jnp.int32,(8,128),1)+uc
    v0=jnp.where((ic>=0)&(ic<128),1.0-fc,0.0); v1=jnp.where((ic>=-1)&(ic<127),fc,0.0)
    c4=uc==2; c2=(uc==0)|(uc==1); c1=(uc==-1)|(uc==1)
    vals=[]
    for kz in range(6):
        g0=[];g1=[]
        for kc in range(6):
            src=TL[kc,pl.ds(pl.multiple_of((z+kz+2)*8,8),8),:]
            g0.append(jnp.take_along_axis(src,i0,axis=0)); g1.append(jnp.take_along_axis(src,i1,axis=0))
        a0,b0=pick2(g0,c4,c2,c1); a1,b1=pick2(g1,c4,c2,c1)
        a=w0*a0+w1*a1; b=w0*b0+w1*b1
        vals.append(v0*a+v1*b)
    z4=uz==2; z2=(uz==0)|(uz==1); z1=(uz==-1)|(uz==1)
    p,q=pick2(vals,z4,z2,z1)
    return p+fz*(q-p)

def split_dot(x,bb):
    hi=x.astype(BF); lo=(x-hi.astype(F32)).astype(BF)
    return jnp.dot(jnp.concatenate([hi,lo],axis=1),bb,preferred_element_type=F32)

def gather_rows(T,g0,n):
    return jnp.concatenate([T[pl.ds(pl.multiple_of(r*EZ+(g0+g)*8,8),8),:] for g in range(n) for r in range(8)],axis=0)

def put_rows(SW,f,g0,n,y,window):
    for g in range(n):
        x=[y[(g*8+r)*8:(g*8+r+1)*8,:] for r in range(8)]
        if window:
            p=x[3]+x[4]; A=x[0]+x[1]+x[2]; B=x[5]+x[6]+x[7]
            r0=A+p; r1=r0+x[5]; r2=r1+x[6]; r3=r2+x[7]; r7=p+B; r6=r7+x[2]; r5=r6+x[1]
            x=[r0,r1,r2,r3,r3,r5,r6,r7]
        for r in range(8):
            SW[f,pl.ds((g0+g)*64+r,8,stride=8),:]=x[r]

def sums_J(JT,b2,bb,SW,g0,n):
    J=gather_rows(JT,g0,n)
    put_rows(SW,1,g0,n,jnp.dot(J.astype(BF),b2[:,0:128],preferred_element_type=F32),True)
    put_rows(SW,3,g0,n,split_dot(J*J,bb[...]),True)

def sums_I(WT,JT,b2,bb,SW,g0,n):
    J=gather_rows(JT,g0,n); I=gather_rows(WT,g0,n)
    y=jnp.dot(I.astype(BF),b2[...],preferred_element_type=F32)
    put_rows(SW,0,g0,n,y[:,0:128],True)
    put_rows(SW,5,g0,n,y[:,128:256],False)
    put_rows(SW,2,g0,n,split_dot(I*I,bb[...]),True)
    put_rows(SW,4,g0,n,split_dot(I*J,bb[...]),True)

def force_group(SW,WZ,JZ,FO,lo_edge,hi_edge,h):
    rows=lax.broadcasted_iota(jnp.int32,(8,128),0)
    inv=1.0/729.0
    def sl(ref,f,zi): return ref[f,pl.ds(pl.multiple_of(zi*8,8),8),:]
    q0=h*8
    S=[]
    for f in range(5):
        x=[sl(SW,f,q0+j) for j in range(16)]
        s2=[x[j]+x[j+1] for j in range(15)]
        s4=[s2[j]+s2[j+2] for j in range(13)]
        S.append([(s4[j]+s4[j+4]+x[j+8])*inv for j in range(8)])
    for j in range(8):
        q=q0+j
        mI,mJ,mII,mJJ,mIJ=[S[f][j] for f in range(5)]
        I=WZ[pl.ds(pl.multiple_of((q+4)*8,8),8),:]; J=JZ[pl.ds(pl.multiple_of((q+4)*8,8),8),:]
        vI=mII-mI*mI; vJ=mJJ-mJ*mJ; cv=mIJ-mI*mJ
        fac=((J-mJ)-cv/(vI+EPS)*(I-mI))*lax.rsqrt(vI*vJ+EPS)
        dead=jnp.logical_or(jnp.logical_and(lo_edge,q<4),jnp.logical_and(hi_edge,q>=NS+4))
        fac=fac*jnp.where(dead,0.0,1.0)
        hf=0.5*fac
        up=WZ[pl.ds(pl.multiple_of((q+5)*8,8),8),:]; dn=WZ[pl.ds(pl.multiple_of((q+3)*8,8),8),:]
        rp=jnp.where(rows==7,0.0,jnp.take_along_axis(I,jnp.minimum(rows+1,7),axis=0))
        rm=jnp.where(rows==0,0.0,jnp.take_along_axis(I,jnp.maximum(rows-1,0),axis=0))
        gc=sl(SW,5,q+4)
        qs=pl.ds(pl.multiple_of(q*8,8),8)
        FO[0,qs,:]=hf*(up-dn); FO[1,qs,:]=hf*(rp-rm); FO[2,qs,:]=fac*gc

def smooth_z(FO,SZ,taps,h):
    for c in range(3):
        x=[FO[c,pl.ds(pl.multiple_of(h*64+j*8,8),8),:] for j in range(16)]
        for j in range(8):
            y=taps[4]*x[j+4]
            for k in range(1,5): y=y+taps[4+k]*(x[j+4-k]+x[j+4+k])
            SZ[c,pl.ds(h*8+j,8,stride=NS),:]=y

def smooth_rc(SZ,gg,glo,put_out,taps,c,hs):
    ys=[]
    for h in hs:
        x=[SZ[c,pl.ds(pl.multiple_of(r*NS+h*8,8),8),:] for r in range(8)]
        for r in range(8):
            y=taps[4]*x[r]
            for k in range(1,5):
                if r-k>=0 and r+k<8: y=y+taps[4+k]*(x[r-k]+x[r+k])
                elif r-k>=0: y=y+taps[4+k]*x[r-k]
                elif r+k<8: y=y+taps[4+k]*x[r+k]
            ys.append(y)
    Y=jnp.concatenate(ys,axis=0)
    hi=Y.astype(BF); lo=(Y-hi.astype(F32)).astype(BF)
    o=jnp.dot(jnp.concatenate([hi,lo],axis=1),gg[...],preferred_element_type=F32)+jnp.dot(hi,glo[...],preferred_element_type=F32)
    for i,h in enumerate(hs):
        for r in range(8):
            put_out(c,pl.ds(h*64+r,8,stride=8),o[i*64+r*8:i*64+(r+1)*8,:])

def loop(n,f,unroll=1):
    def g(i,_):
        f(i); return 0
    lax.fori_loop(0,n,g,0,unroll=unroll)

def interior(WT,JT,WZ,JZ,b2,bb,gg,glo,SW,FO,SZ,put_out,taps,lo_edge,hi_edge):
    loop(4,lambda i: sums_I(WT,JT,b2,bb,SW,1+2*i,2))
    loop(7,lambda i: force_group(SW,WZ,JZ,FO,lo_edge,hi_edge,1+i))
    loop(6,lambda i: smooth_z(FO,SZ,taps,1+i))
    loop(3,lambda c: smooth_rc(SZ,gg,glo,put_out,taps,c,range(1,7)))

def rim(WT,JT,WZ,JZ,b2,bb,gg,glo,SW,FO,SZ,put_out,taps,lo_edge,hi_edge):
    loop(2,lambda i: sums_I(WT,JT,b2,bb,SW,9*i,1),unroll=2)
    loop(2,lambda i: force_group(SW,WZ,JZ,FO,lo_edge,hi_edge,8*i))
    loop(2,lambda i: smooth_z(FO,SZ,taps,7*i),unroll=2)
    loop(3,lambda c: smooth_rc(SZ,gg,glo,put_out,taps,c,(0,7)),unroll=3)


MESH = pl.DeviceIdType.MESH
NG = 4
MEMBERS = 64
LOW = 2
HIGH = 3
BASE = 4
CH = 16
FAR = (2, 3, 1, 0)


def remote(src, dst, ssem, rsem, dev):
    return pltpu.make_async_remote_copy(src_ref=src, dst_ref=dst, send_sem=ssem, recv_sem=rsem, device_id=dev, device_id_type=MESH)


def kernel(taps, tmpl, subj_h, sh_h, fr_h, cst, vel, tf,
           b2, bb, gg, glo, tpl, subj, sh, fr, SH, WH, WBF, RBJ, RBW, TL, WT, JT, WZ, JZ, SW, FO, SZ,
           csem, lsem, tsend, trecv, tlow, thigh, hsend, hrecv, wsend, wrecv, rsend, rrecv, jsend, jrecv, xs):
    gz = lax.axis_index("gz")
    me = lax.axis_index("subj")
    has_lo = gz > 0
    has_hi = gz < NG - 1
    one = lambda b: b.astype(jnp.int32)
    own = tpl.at[pl.ds(BASE + me, 1)]
    c0 = me // 4
    c_t = pltpu.make_async_copy(tmpl, own, lsem.at[0])
    c_s = pltpu.make_async_copy(subj_h.at[0], subj, lsem.at[1])
    c_h = pltpu.make_async_copy(sh_h.at[0], sh, lsem.at[2])
    c_f = pltpu.make_async_copy(fr_h.at[0], fr, lsem.at[3])
    pieces = ((0, 256, b2), (0, 128, bb.at[0:128]), (0, 128, bb.at[128:256]),
              (256, 128, gg.at[0:128]), (256, 128, gg.at[128:256]), (384, 128, glo))
    c_c = [pltpu.make_async_copy(cst.at[:, a:a + n], d, csem.at[i]) for i, (a, n, d) in enumerate(pieces)]
    c_t.start()

    bar = pltpu.get_barrier_semaphore()

    def signal(dev):
        pl.semaphore_signal(bar, inc=1, device_id=dev, device_id_type=MESH)

    px, pz, py = me // 16, lax.rem(me // 4, 4), lax.rem(me, 4)
    at_x = [lax.rem(px + d, 4) * 16 for d in range(4)]
    at_z = [lax.rem(pz + d, 4) * 4 for d in range(4)]
    at_y = [lax.rem(py + d, 4) for d in range(4)]
    peers = [at_x[a] + at_z[b] + at_y[d] for a in FAR for b in FAR for d in FAR if a + b + d > 0]
    for p in peers:
        signal((gz, p))

    @pl.when(has_lo)
    def _():
        for k in range(LOW):
            signal((gz - 1, MEMBERS - LOW + k))

    @pl.when(has_hi)
    def _():
        signal((gz + 1, me))
        for k in range(HIGH):
            signal((gz + 1, k))
    sends_up = jnp.logical_and(has_hi, me >= MEMBERS - LOW)
    sends_dn = jnp.logical_and(has_lo, me < HIGH)

    for c in (c_s, *c_c[0:3], c_h, c_f, *c_c[3:]):
        c.start()

    for ref in (WT, JT, WZ, JZ):
        def zero(r, _):
            a = pl.ds(pl.multiple_of(r * EZ, 8), 8)
            b = pl.ds(pl.multiple_of(r * EZ + EZ - 8, 8), 8)
            ref[a, :] = jnp.zeros((8, 128), F32)
            ref[b, :] = jnp.zeros((8, 128), F32)
            return 0
        if ref is WT or ref is JT:
            lax.fori_loop(0, 8, zero, 0)
        else:
            ref[0:64, :] = jnp.zeros((64, 128), F32)
            ref[EZ * 8 - 64:EZ * 8, :] = jnp.zeros((64, 128), F32)

    @pl.when(jnp.logical_not(has_lo))
    def _():
        tpl[BASE - LOW:BASE] = jnp.zeros((LOW, 8, 128), BF)

    @pl.when(jnp.logical_not(has_hi))
    def _():
        tpl[BASE + NS:BASE + NS + HIGH] = jnp.zeros((HIGH, 8, 128), BF)
    tpl[0:BASE - LOW] = jnp.zeros((BASE - LOW, 8, 128), BF)
    tpl[BASE + NS + HIGH:TZ] = jnp.zeros((TZ - BASE - NS - HIGH, 8, 128), BF)

    def put(T, Z, zi, v):
        T[pl.ds(zi, 8, stride=EZ), :] = v
        Z[pl.ds(pl.multiple_of(zi * 8, 8), 8), :] = v

    def subject_sums():
        loop(NS, lambda z: put(JT, JZ, z + 8, subj[z].astype(F32)), unroll=4)
        for c in c_c:
            c.wait()
        loop(4, lambda i: sums_J(JT, b2, bb, SW, 1 + 2 * i, 2))
    dist = jnp.minimum(px, 4 - px) + jnp.minimum(py, 4 - py) + jnp.where(gz < 2, pz, 4 - pz)
    early = dist < 6

    @pl.when(early)
    def _():
        c_s.wait()
        subject_sums()

    c_t.wait()
    pl.semaphore_wait(bar, MEMBERS - 1 + one(has_lo) + MEMBERS * (one(sends_up) + one(sends_dn)))

    @pl.when(sends_up)
    def _():
        def f(i, _):
            remote(own, tpl.at[pl.ds(BASE - LOW + me - (MEMBERS - LOW), 1)], hsend.at[2], tlow, (gz + 1, i)).start()
            return 0
        lax.fori_loop(0, MEMBERS, f, 0)

    @pl.when(sends_dn)
    def _():
        def f(i, _):
            remote(own, tpl.at[pl.ds(BASE + NS + me, 1)], hsend.at[3], thigh, (gz - 1, i)).start()
            return 0
        lax.fori_loop(0, MEMBERS, f, 0)

    for p in peers:
        remote(own, own, tsend, trecv.at[c0], (gz, p)).start()

    s_dn = remote(subj.at[0:8], SH.at[1], hsend.at[0], hrecv.at[1], (gz - 1, me))
    s_up = remote(subj.at[NS - 8:NS], SH.at[0], hsend.at[1], hrecv.at[0], (gz + 1, me))
    w_dn = remote(WBF.at[0:8], WH.at[1], wsend.at[0], wrecv.at[1], (gz - 1, me))
    w_up = remote(WBF.at[NS - 8:NS], WH.at[0], wsend.at[1], wrecv.at[0], (gz + 1, me))


    @pl.when(has_lo)
    def _():
        pl.semaphore_signal(xs, inc=1, device_id=(gz - 1, me), device_id_type=MESH)
    @pl.when(jnp.logical_not(early))
    def _():
        c_s.wait()

    @pl.when(has_lo)
    def _():
        s_dn.start()

    for p in peers:
        remote(subj.at[p], RBJ.at[me], jsend, jrecv, (gz, p)).start()

    def halos(H, T, Z, sems):
        @pl.when(has_lo)
        def _():
            pltpu.make_async_copy(H.at[0], H.at[0], sems.at[0]).wait()

            def f(i, _):
                put(T, Z, i, H[0, i].astype(F32))
                return 0
            lax.fori_loop(0, 8, f, 0)

        @pl.when(has_hi)
        def _():
            pltpu.make_async_copy(H.at[1], H.at[1], sems.at[1]).wait()

            def f(i, _):
                put(T, Z, NS + 8 + i, H[1, i].astype(F32))
                return 0
            lax.fori_loop(0, 8, f, 0)
    c_h.wait()
    c_f.wait()

    def prepare(e, fresh):
        in_slab = jnp.logical_and(fresh, jnp.logical_and(e >= 0, e < CH))
        ei = jnp.maximum(jnp.minimum(e, CH - 1), 0)

        @pl.when(jnp.logical_and(e < 0, has_lo))
        def _():
            pltpu.make_async_copy(tpl.at[0:LOW], tpl.at[0:LOW], tlow).wait()

        @pl.when(jnp.logical_and(e >= CH, has_hi))
        def _():
            pltpu.make_async_copy(tpl.at[0:HIGH], tpl.at[0:HIGH], thigh).wait()

        @pl.when(jnp.logical_and(in_slab, e == c0))
        def _():
            pltpu.make_async_copy(tpl.at[0:3], tpl.at[0:3], trecv.at[ei]).wait()

        @pl.when(jnp.logical_and(in_slab, e != c0))
        def _():
            pltpu.make_async_copy(tpl.at[0:4], tpl.at[0:4], trecv.at[ei]).wait()
        lane_shift(tpl, TL, e + 1, 1)

    rising = gz == 2

    def place(k):
        w = jnp.where(k < 2, 12 + k, jnp.where(k < CH - 2, k - 2, k))
        e = jnp.where(k < 2, 13 + k, jnp.where(k == 2, -1, jnp.where(k < 12, k - 1, jnp.where(k < CH - 2, 10, k + 1))))
        fresh = jnp.logical_or(rising, jnp.logical_or(k < 12, k >= CH - 2))
        return jnp.where(rising, k, w), jnp.where(rising, k + 1, e), fresh

    beside = me - py + lax.rem(py + 1, 4)

    def after(w):
        for j in range(4):
            z = 4 * w + j
            mine = z == me
            to = jnp.where(mine, beside, z)
            remote(WBF.at[z], RBW.at[jnp.where(mine, MEMBERS, me)], rsend, rrecv, (gz, to)).start()

        @pl.when(jnp.logical_and(has_lo, w == 1))
        def _():
            w_dn.start()

        @pl.when(jnp.logical_and(has_hi, w == CH - 1))
        def _():
            w_up.start()

    def wp(k):
        w, e, fresh = place(k)
        prepare(e, fresh)
        for j in range(4):
            z = 4 * w + j
            v = warp_slice(z, sh, fr, TL).astype(BF)
            WBF[z] = v
            put(WT, WZ, z + 8, v.astype(F32))

        @pl.when(k > 0)
        def _():
            after(place(k - 1)[0])

    def begin(i):
        @pl.when(jnp.logical_or(i < 2, jnp.logical_not(rising)))
        def _():
            prepare(jnp.where(rising, -i, jnp.where(i < 2, 11 + i, i - 2)), True)
    loop(4, begin)
    loop(CH - 1, wp)

    @pl.when(has_hi)
    def _():
        pl.semaphore_wait(xs, 1)
        s_up.start()
    wp(CH - 1)
    after(place(CH - 1)[0])

    @pl.when(jnp.logical_not(early))
    def _():
        subject_sums()

    RBW[me] = WBF[me]
    RBJ[me] = subj[me]

    def put_out(c, rows, v):
        vel[0, c, rows, :] = v
    A = (WT, JT, WZ, JZ, b2, bb, gg, glo, SW, FO, SZ, put_out, taps, jnp.logical_not(has_lo), jnp.logical_not(has_hi))
    interior(*A)
    halos(SH, JT, JZ, hrecv)
    loop(2, lambda i: sums_J(JT, b2, bb, SW, 9 * i, 1))
    halos(WH, WT, WZ, wrecv)
    rim(*A)

    def total(R, n, sem):
        pltpu.make_async_copy(R.at[0:n], R.at[0:n], sem).wait()
        parts = [R[i].astype(F32) for i in range(MEMBERS)]
        while len(parts) > 1:
            parts = [a + b for a, b in zip(parts[0::2], parts[1::2])]
        return parts[0]
    tf[0] = (total(RBJ, MEMBERS - 1, jrecv) - total(RBW, MEMBERS, rrecv)) * (1.0 / 8.0)

    pltpu.make_async_copy(tpl.at[0:MEMBERS - 1], tpl.at[0:MEMBERS - 1], tsend).wait()
    pltpu.make_async_copy(RBW.at[0:MEMBERS], RBW.at[0:MEMBERS], rsend).wait()
    pltpu.make_async_copy(RBJ.at[0:MEMBERS - 1], RBJ.at[0:MEMBERS - 1], jsend).wait()

    @pl.when(sends_up)
    def _():
        pltpu.make_async_copy(tpl.at[0:MEMBERS], tpl.at[0:MEMBERS], hsend.at[2]).wait()

    @pl.when(sends_dn)
    def _():
        pltpu.make_async_copy(tpl.at[0:MEMBERS], tpl.at[0:MEMBERS], hsend.at[3]).wait()

    @pl.when(has_lo)
    def _():
        s_dn.wait_send()
        w_dn.wait_send()

    @pl.when(has_hi)
    def _():
        s_up.wait_send()
        w_up.wait_send()


def write_out(a, b, vel, tf, sem):
    copies = [pltpu.make_async_copy(a.at[:, i], vel.at[:, i], sem.at[i]) for i in range(3)]
    copies.append(pltpu.make_async_copy(b, tf, sem.at[3]))
    for c in copies:
        c.start()
    for c in copies:
        c.wait()


def per_device(template, subjects, shifts, fractions):
    cst, taps = packed_constants()
    V = pltpu.VMEM
    D = pltpu.SemaphoreType.DMA
    hbm = pl.BlockSpec(memory_space=pltpu.HBM)
    vm = pl.BlockSpec(memory_space=pltpu.VMEM)
    shapes = (jax.ShapeDtypeStruct((1, 3, 512, 128), F32), jax.ShapeDtypeStruct((1, 8, 128), F32))
    operands = [pltpu.with_memory_space_constraint(a, pltpu.HBM) for a in (template, subjects, shifts, fractions, jnp.asarray(cst))]
    vel, tf = pl.pallas_call(
        functools.partial(kernel, taps),
        out_shape=shapes,
        in_specs=[hbm] * 5,
        out_specs=[vm] * 2,
        scratch_shapes=[
            V((128, 256), BF), V((256, 128), BF), V((256, 128), BF), V((128, 128), BF),
            V((TZ, 8, 128), BF), V((64, 8, 128), BF), V((3, 64, 8, 128), jnp.int32), V((3, 64, 8, 128), BF),
            V((2, 8, 8, 128), BF), V((2, 8, 8, 128), BF),
            V((64, 8, 128), BF), V((64, 8, 128), BF), V((65, 8, 128), BF),
            V((6, TZ * 8, 128), F32), V((640, 128), F32), V((640, 128), F32), V((640, 128), F32), V((640, 128), F32),
            V((6, 640, 128), F32), V((3, 576, 128), F32), V((3, 512, 128), F32),
            D((6,)), D((4,)), D(()), D((CH,)), D(()), D(()), D((4,)), D((2,)), D((2,)), D((2,)), D(()), D(()), D(()), D(()), pltpu.SemaphoreType.REGULAR,
        ],
        compiler_params=pltpu.CompilerParams(collective_id=0, has_side_effects=True, vmem_limit_bytes=32 << 20),
    )(*operands)
    vel, tf = pl.pallas_call(
        write_out,
        out_shape=shapes,
        in_specs=[vm] * 2,
        out_specs=[hbm] * 2,
        scratch_shapes=[D((4,))],
        compiler_params=pltpu.CompilerParams(vmem_limit_bytes=4 << 20),
    )(vel, tf)
    return vel.reshape(1, 3, 64, 8, 128), tf


def solution(mesh):
    placed = (
        P(("gz", "subj"), None, None),
        P("subj", "gz", None, None),
        P("subj", None, "gz", None, None),
        P("subj", None, "gz", None, None),
    )
    return jax.shard_map(
        per_device,
        mesh=mesh,
        in_specs=placed,
        out_specs=(P("subj", None, "gz", None, None), P(("gz", "subj"), None, None)),
        check_vma=False,
    )
```
